512 devices in a mesh: tile: 64 (over x, z_lo, core), agent: 8 (over z_hi, y).
Axes of the slice: x: 4, y: 4, z: 16 (z_hi: 2, z_lo: 8; z = z_hi * 8 + z_lo), core: 2. Of those that a mesh axis runs over, the one named last changes fastest.
Arguments:
- states: float32 [8, 8, 128, 256], P('agent', None, 'tile'), may hold values from -6 to 6
- footprints: float32 [64, 64, 64, 512], P('agent', 'tile'), may hold values from -0.25 to 0.25
- offsets: int32 [64, 64], P('agent', 'tile'), may hold values from 0 to 1984, as said below
- measured: float32 [64, 8, 2048], P('agent', None, 'tile'), may hold values from -9 to 9
- weights: float32 [64, 8, 2048], P('agent', None, 'tile'), may hold values from 0.2 to 5
Outputs:
- new_states: float32 [8, 8, 128, 256], P('agent', None, 'tile')
- prior_volume: float32 [8, 128, 256], P(None, 'tile')
The draws below stay inside these ranges and needn't reach their ends.
Inputs may be any that keep to these rules, and one draw needn't show every extreme that they name: For one agent and one tile t, the values offsets[v, t] // 32 differ between the agent's 8 views v.
All inputs are finite; a program needn't handle non-finite values.
Results may differ from the reference program's by a relative error of at most 0.0003.
Values sent between devices are 32-bit elements; how exact they have to be, the bound alone decides.
No kernel may reach another device: no remote copies, remote signals or barrier semaphores. Data moves between devices by JAX's collectives and lax.ppermute only.
A program may use at most 64 MiB of HBM per device.

```python
import math
import jax
import jax.numpy as jnp
from jax import lax

SL = 8
COLS = 256
V_AG = 8
FOOT = 64
DET = 2048
ITERS = 1
SWEEPS = 2
PIX_DEV = 512
ROWS = 128
AGENTS = 8
TILES = 64
VIEWS = 64


def draw_offsets(key, part):
    share = DET // TILES
    start_count = (DET - FOOT) // share + 1
    score_key = jax.random.fold_in(key, 11)
    shift_key = jax.random.fold_in(key, 23)
    scores = jax.random.randint(score_key, (AGENTS, TILES, start_count), 0, 2 ** 18, dtype=jnp.int32)
    scores = scores * start_count + jnp.arange(start_count, dtype=jnp.int32)[None, None, :]
    order = jnp.argsort(scores, axis=-1, stable=True)[:, :, :V_AG].astype(jnp.int32)
    base = order * share
    upper = jnp.minimum(share, DET - FOOT - base + 1)
    extra = jax.random.randint(shift_key, (AGENTS, TILES, V_AG), 0, upper, dtype=jnp.int32)
    placed = (base + extra).transpose(0, 2, 1)
    return placed.reshape(AGENTS * V_AG, TILES).astype(jnp.int32)


def shard_levels(own_key, dims, shards, smallest, high):
    factor_of = 1.0
    for position, shards_of in shards:
        heights = jax.random.uniform(jax.random.fold_in(jax.random.fold_in(own_key, 6), position), (shards_of,), jnp.float32, smallest / len(shards), high / len(shards))
        factor_of = factor_of * jnp.repeat(jnp.exp(heights), dims[position] // shards_of).reshape((-1,) + (1,) * (len(dims) - 1 - position))
    return factor_of


def bell_draw(rng, extent, deviation, reach, cuts=(), kind=jnp.bfloat16):
    level = shard_levels(rng, extent, cuts, -0.22, 0.18) if cuts else 1.0
    result = jax.random.normal(rng, extent, jnp.float32) * deviation * level
    return jnp.minimum(jnp.maximum(result, -reach), reach).astype(kind)


def setup_inputs(seed: int = 0) -> dict:
    keys = jax.random.split(jax.random.key(seed), 6)
    return {
        "states": bell_draw(keys[0], (AGENTS, SL, ROWS, COLS), 1.0, 6.0, ((0, 8), (2, 64)), jnp.float32),
        "footprints": bell_draw(keys[1], (VIEWS, TILES, FOOT, PIX_DEV), PIX_DEV ** -0.5, 0.25, ((0, 8), (1, 64)), jnp.float32),
        "offsets": draw_offsets(jax.random.fold_in(keys[5], 71), 0),
        "measured": bell_draw(keys[3], (VIEWS, SL, DET), 1.5, 9.0, ((0, 8), (2, 64)), jnp.float32),
        "weights": jnp.clip(jnp.exp(math.log(5.0) - 3.218876 * jax.random.uniform(keys[4], (VIEWS, SL, DET), jnp.float32) ** shard_levels(keys[4], (VIEWS, SL, DET), ((0, 8), (2, 64)), -0.2, 0.2)), 0.2, 5.0),
    }


STEP_SIZE = 0.25
RELAX = 0.6
QRATIO = 0.6


def neighbour_table():
    offsets_nb = []
    for a in (-1, 0, 1):
        for b in (-1, 0, 1):
            for c in (-1, 0, 1):
                if a != 0 or b != 0 or c != 0:
                    offsets_nb.append((a, b, c, 1.0 / ((a * a + b * b + c * c) ** 0.5)))
    total = sum(item[3] for item in offsets_nb)
    return [(a, b, c, 4.0 * w / total) for (a, b, c, w) in offsets_nb]


def sweep_update(padded, average):
    depth, height, width = average.shape
    centre = padded[1:1 + depth, 1:1 + height, 1:1 + width]
    numerator = average
    denominator = jnp.ones_like(average)
    for (a, b, c, weight_nb) in neighbour_table():
        neighbour = padded[1 + a:1 + a + depth, 1 + b:1 + b + height, 1 + c:1 + c + width]
        differ = centre - neighbour
        powered = jnp.power(differ * differ, 0.4)
        coefficient = weight_nb * (1.0 + QRATIO * powered) / ((1.0 + powered) * (1.0 + powered))
        numerator = numerator + coefficient * neighbour
        denominator = denominator + coefficient
    return numerator / denominator


def data_step(packed):
    current, blocks, offsets_ag, measured_ag, weights_ag = packed
    slices = current.shape[0]
    tiles = blocks.shape[1]
    foot = blocks.shape[2]
    pixels = blocks.shape[3]
    detector = measured_ag.shape[2]
    volume = current.reshape(slices, tiles, pixels).transpose(1, 0, 2)
    projected = jnp.einsum('tsp,vtbp->vtbs', volume, blocks, precision=lax.Precision.HIGHEST)
    bin_index = offsets_ag.astype(jnp.int32)[:, :, None] + jnp.arange(foot, dtype=jnp.int32)[None, None, :]

    def place(index_view, values_view):
        empty = jnp.zeros((detector, slices), values_view.dtype)
        return empty.at[index_view.reshape(-1)].add(values_view.reshape(-1, slices))

    sinogram = jax.vmap(place)(bin_index, projected).transpose(0, 2, 1)
    residual = weights_ag * (sinogram - measured_ag)
    residual_t = residual.transpose(0, 2, 1)

    def take(rows_view, index_view):
        return rows_view[index_view]

    windows = jax.vmap(take)(residual_t, bin_index)
    gradient = jnp.einsum('vtbs,vtbp->tsp', windows, blocks, precision=lax.Precision.HIGHEST)
    gradient = gradient.transpose(1, 0, 2).reshape(current.shape)
    return current - STEP_SIZE * gradient


def reference(states, footprints, offsets, measured, weights):
    agents = states.shape[0]
    views = footprints.shape[0] // agents
    blocks = footprints.reshape((agents, views) + footprints.shape[1:])
    offsets_all = offsets.reshape(agents, views, offsets.shape[1])
    measured_all = measured.reshape((agents, views) + measured.shape[1:])
    weights_all = weights.reshape((agents, views) + weights.shape[1:])
    current = states
    prior_vol = states[0]
    for repeat in range(ITERS):
        fitted = lax.map(data_step, (current, blocks, offsets_all, measured_all, weights_all))
        reflect = 2.0 * fitted - current
        average = jnp.sum(reflect, axis=0) / agents
        volume = average
        for sweep_index in range(SWEEPS):
            volume = sweep_update(jnp.pad(volume, 1), average)
        prior_vol = volume
        current = (1.0 - RELAX) * current + RELAX * (2.0 * prior_vol[None] - reflect)
    return current, prior_vol
```

```python
import jax
import jax.numpy as jnp
from jax import lax
from jax.experimental import pallas as pl
from jax.experimental.pallas import tpu as pltpu
from jax.sharding import PartitionSpec as P

SWEEPS = 2
STEP_SIZE = 0.25
RELAX = 0.6
QRATIO = 0.6
BLOCK = 32
LANES = 128

SMEM = pl.BlockSpec(memory_space=pltpu.SMEM)
VMEM = pl.BlockSpec(memory_space=pltpu.VMEM)


def neighbour_table():
    offsets_nb = []
    for a in (-1, 0, 1):
        for b in (-1, 0, 1):
            for c in (-1, 0, 1):
                if a != 0 or b != 0 or c != 0:
                    offsets_nb.append((a, b, c, 1.0 / (a * a + b * b + c * c) ** 0.5))
    total = sum((item[3] for item in offsets_nb))
    return [(a, b, c, 4.0 * w / total) for a, b, c, w in offsets_nb]


def halves(x):
    high = x.astype(jnp.bfloat16)
    return high, (x - high.astype(jnp.float32)).astype(jnp.bfloat16)


def split_dot(small, large, dims):
    rows = small.shape[0]
    stacked = jnp.concatenate([x.astype(jnp.float32) for x in halves(small)], axis=0).astype(jnp.bfloat16)
    total = None
    for part in halves(large):
        both = lax.dot_general(stacked, part, (dims, ((), ())), preferred_element_type=jnp.float32)
        both = both[:rows] + both[rows:]
        total = both if total is None else total + both
    return total


def lane_iota(shape):
    return lax.broadcasted_iota(jnp.int32, shape, len(shape) - 1)


def project_kernel(offsets_ref, states_ref, blocks_ref, measured_ref, weights_ref, out_ref):
    views, _, foot, pixels = blocks_ref.shape
    slices, width = states_ref.shape[1], states_ref.shape[3]
    share = measured_ref.shape[2]
    lane = lane_iota((slices, LANES))
    blocks = blocks_ref[:, 0].reshape(views * foot, pixels)
    projected = split_dot(states_ref[0, :, 0, :], blocks[:, :width], ((1,), (1,)))
    projected += split_dot(states_ref[0, :, 1, :], blocks[:, width:], ((1,), (1,)))
    step = pl.program_id(0)
    per_vreg = LANES // foot
    blank = jnp.zeros((slices, LANES - share), jnp.float32)
    for local in range(views):
        view = step * views + local
        offset = offsets_ref[view, 0]
        base = offset // BLOCK
        shift = offset - base * BLOCK
        at = (local % per_vreg) * foot
        pair = projected[:, (local // per_vreg) * LANES : (local // per_vreg + 1) * LANES]
        band = jnp.where((lane >= at) & (lane < at + foot), pair, 0.0)
        band = pltpu.roll(band, (shift + LANES - at) % LANES, 1)
        first = band + jnp.concatenate([blank, measured_ref[local]], axis=1)
        second = jnp.concatenate([weights_ref[local], blank], axis=1)
        second = jnp.where(lane == share, base.astype(jnp.float32), second)
        start = view * 2 * slices
        out_ref[pl.ds(start, slices, stride=2), :] = first
        out_ref[pl.ds(start + 1, slices, stride=2), :] = second


def residual_kernel(in_ref, out_ref):
    tiles = out_ref.shape[0]
    share = BLOCK
    lane = lane_iota((tiles, LANES))
    first = in_ref[pl.ds(0, tiles, stride=2), :]
    second = in_ref[pl.ds(1, tiles, stride=2), :]
    base = second[:, share : share + 1].astype(jnp.int32)
    onehot = jnp.where(lane_iota((tiles, tiles)) == base, 1.0, 0.0)
    placed = lax.dot_general(
        onehot, first, (((0,), (0,)), ((), ())), precision=lax.Precision.HIGHEST, preferred_element_type=jnp.float32
    )
    total = placed
    for part in (1, 2):
        moved = pltpu.roll(placed, part, 0)
        total += pltpu.roll(moved, LANES - part * share, 1)
    measured = pltpu.roll(first, share, 1)
    residual = jnp.where(lane < share, second * (total - measured), 0.0)
    windows = residual
    for part in (1, 2):
        moved = pltpu.roll(residual, tiles - part, 0)
        windows += pltpu.roll(moved, part * share, 1)
    out_ref[...] = jnp.dot(onehot, windows, precision=lax.Precision.HIGHEST, preferred_element_type=jnp.float32)


def gradient_kernel(offsets_ref, windows_ref, states_ref, blocks_ref, out_ref):
    views, _, foot, pixels = blocks_ref.shape
    slices, width = states_ref.shape[1], states_ref.shape[3]
    copies = out_ref.shape[0]
    lane = lane_iota((slices, LANES))
    per_vreg = LANES // foot
    pieces = []
    for view in range(views):
        offset = offsets_ref[view, 0]
        shift = offset - (offset // BLOCK) * BLOCK
        at = (view % per_vreg) * foot
        window = windows_ref[view * slices : (view + 1) * slices, :]
        window = pltpu.roll(window, (LANES + at - shift) % LANES, 1)
        if at == 0:
            pieces.append(window)
        else:
            pieces[-1] = jnp.where(lane >= at, window, pieces[-1])
    windows = jnp.concatenate(pieces, axis=1)
    blocks = blocks_ref[:, 0].reshape(views * foot, pixels)
    gradient = split_dot(windows, blocks, ((1,), (0,)))
    for row in range(2):
        at = slice(row * width, (row + 1) * width)
        reflect = states_ref[0, :, row, :] - (2.0 * STEP_SIZE) * gradient[:, at]
        for copy in range(copies):
            out_ref[copy, :, at] = reflect


def mean_kernel(in_ref, out_ref):
    count = in_ref.shape[0]
    total = in_ref[0]
    for agent in range(1, count):
        total = total + in_ref[agent]
    out_ref[...] = total * (1.0 / count)


def shifted(row, a, c):
    slices, width = row.shape
    if a:
        where = lax.broadcasted_iota(jnp.int32, row.shape, 0)
        row = pltpu.roll(row, (slices - a) % slices, 0)
        row = jnp.where(where == (slices - 1 if a > 0 else 0), 0.0, row)
    if c:
        where = lane_iota(row.shape)
        row = pltpu.roll(row, (width - c) % width, 1)
        row = jnp.where(where == (width - 1 if c > 0 else 0), 0.0, row)
    return row


def sweep_rows(rows, averages):
    table = neighbour_table()
    moved = [{(a, c): shifted(row, a, c) for a in (-1, 0, 1) for c in (-1, 0, 1)} for row in rows]
    out = []
    for index, average in enumerate(averages):
        centre = rows[index + 1]
        numerator = average
        denominator = jnp.ones_like(average)
        for a, b, c, weight_nb in table:
            neighbour = moved[index + 1 + b][(a, c)]
            differ = centre - neighbour
            powered = jnp.exp(0.4 * jnp.log(differ * differ))
            above = 1.0 + powered
            coefficient = (weight_nb + (weight_nb * QRATIO) * powered) / (above * above)
            numerator = numerator + coefficient * neighbour
            denominator = denominator + coefficient
        out.append(numerator / denominator)
    return out


def prior_kernel(where_ref, mean_ref, near_ref, side_ref, states_ref, reflect_ref, new_ref, prior_ref):
    width = states_ref.shape[3]
    tile = where_ref[0]
    last = where_ref[1]
    odd = tile % 2 == 1
    near = near_ref[...]
    side = side_ref[...]
    mean = mean_ref[...]
    above = jnp.where(odd, near, side)
    below = jnp.where(odd, side, near)
    above = jnp.where(tile == 0, 0.0, above)
    below = jnp.where(tile == last, 0.0, below)
    rows = [x[:, i * width : (i + 1) * width] for x in (above, mean, below) for i in range(2)]
    averages = rows
    swept = sweep_rows(rows, averages[1:5])
    swept[0] = jnp.where(tile == 0, 0.0, swept[0])
    swept[3] = jnp.where(tile == last, 0.0, swept[3])
    final = sweep_rows(swept, averages[2:4])
    for row in range(2):
        reflect = reflect_ref[0, :, row * width : (row + 1) * width]
        prior_ref[:, row, :] = final[row]
        new_ref[0, :, row, :] = (1.0 - RELAX) * states_ref[0, :, row, :] + RELAX * (2.0 * final[row] - reflect)


def halo_pairs(n_tile, n_agent, per_x):
    near, side = [], []
    for tile in range(n_tile):
        for agent in range(n_agent):
            near.append((tile * n_agent + agent, (tile ^ 1) * n_agent + agent))
    for tile in range(1, n_tile - 1, 2):
        other = tile + 1
        for agent in range(n_agent):
            crossing = tile // per_x != other // per_x
            partner = (agent + n_agent // 2) % n_agent if crossing else agent
            one, two = tile * n_agent + agent, other * n_agent + partner
            side += [(one, two), (two, one)]
    return near, side


def shards(states, footprints, offsets, measured, weights):
    n_tile = lax.axis_size("tile")
    n_agent = lax.axis_size("agent")
    _, slices, height, width = states.shape
    views, _, foot, pixels = footprints.shape
    share = measured.shape[2]
    f32 = jnp.float32

    half = views // 2
    sent = pl.pallas_call(
        project_kernel,
        grid=(2,),
        in_specs=[
            SMEM,
            pl.BlockSpec(states.shape, lambda i: (0, 0, 0, 0)),
            pl.BlockSpec((half, 1, foot, pixels), lambda i: (i, 0, 0, 0)),
            pl.BlockSpec((half, slices, share), lambda i: (i, 0, 0)),
            pl.BlockSpec((half, slices, share), lambda i: (i, 0, 0)),
        ],
        out_specs=pl.BlockSpec((2 * n_tile, LANES), lambda i: (0, 0)),
        out_shape=jax.ShapeDtypeStruct((2 * n_tile, LANES), f32),
        name="project",
    )(offsets, states, footprints, measured, weights)
    bands = lax.all_to_all(sent.reshape(n_tile, 2, LANES), "tile", 0, 0, tiled=True)
    back = pl.pallas_call(
        residual_kernel,
        in_specs=[VMEM],
        out_specs=VMEM,
        out_shape=jax.ShapeDtypeStruct((n_tile, LANES), f32),
        name="residual",
    )(bands.reshape(2 * n_tile, LANES))
    windows = lax.all_to_all(back.reshape(n_tile, 1, LANES), "tile", 0, 0, tiled=True)
    copies = pl.pallas_call(
        gradient_kernel,
        in_specs=[SMEM, VMEM, VMEM, VMEM],
        out_specs=VMEM,
        out_shape=jax.ShapeDtypeStruct((n_agent, slices, pixels), f32),
        name="gradient",
    )(offsets, windows.reshape(n_tile, LANES), states, footprints)
    reflects = lax.all_to_all(copies, "agent", 0, 0, tiled=True)
    mean = pl.pallas_call(
        mean_kernel,
        in_specs=[VMEM],
        out_specs=VMEM,
        out_shape=jax.ShapeDtypeStruct((slices, pixels), f32),
        name="mean",
    )(reflects)
    near_pairs, side_pairs = halo_pairs(n_tile, n_agent, 16)
    side = lax.ppermute(mean, ("tile", "agent"), side_pairs)
    near = lax.ppermute(mean, ("tile", "agent"), near_pairs)
    where = jnp.stack([lax.axis_index("tile"), jnp.int32(n_tile - 1)]).astype(jnp.int32)
    new_states, prior = pl.pallas_call(
        prior_kernel,
        grid=(1,),
        in_specs=[
            SMEM,
            pl.BlockSpec((slices, pixels), lambda i: (0, 0)),
            pl.BlockSpec((slices, pixels), lambda i: (0, 0)),
            pl.BlockSpec((slices, pixels), lambda i: (0, 0)),
            pl.BlockSpec(states.shape, lambda i: (0, 0, 0, 0)),
            pl.BlockSpec((1, slices, pixels), lambda i: (0, 0, 0)),
        ],
        out_specs=[
            pl.BlockSpec(states.shape, lambda i: (0, 0, 0, 0)),
            pl.BlockSpec((slices, height, width), lambda i: (0, 0, 0)),
        ],
        out_shape=[
            jax.ShapeDtypeStruct(states.shape, f32),
            jax.ShapeDtypeStruct((slices, height, width), f32),
        ],
        name="prior",
    )(where, mean, near, side, states, copies)
    return new_states, prior


def solution(mesh):
    in_specs = (
        P("agent", None, "tile", None),
        P("agent", "tile", None, None),
        P("agent", "tile"),
        P("agent", None, "tile"),
        P("agent", None, "tile"),
    )
    out_specs = (P("agent", None, "tile", None), P(None, "tile", None))
    return jax.shard_map(shards, mesh=mesh, in_specs=in_specs, out_specs=out_specs, check_vma=False)
```

```python
import jax
import jax.numpy as jnp
from jax import lax
from jax.experimental import pallas as pl
from jax.experimental.pallas import tpu as pltpu
from jax.sharding import PartitionSpec as P

SWEEPS = 2
STEP_SIZE = 0.25
RELAX = 0.6
QRATIO = 0.6
BLOCK = 32
LANES = 128

SMEM = pl.BlockSpec(memory_space=pltpu.SMEM)
VMEM = pl.BlockSpec(memory_space=pltpu.VMEM)


def near(x):
    return pltpu.with_memory_space_constraint(x, pltpu.VMEM)


def near_shape(*shape):
    return pltpu.VMEM(shape, jnp.float32)


def neighbour_table():
    offsets_nb = []
    for a in (-1, 0, 1):
        for b in (-1, 0, 1):
            for c in (-1, 0, 1):
                if a != 0 or b != 0 or c != 0:
                    offsets_nb.append((a, b, c, 1.0 / (a * a + b * b + c * c) ** 0.5))
    total = sum((item[3] for item in offsets_nb))
    return [(a, b, c, 4.0 * w / total) for a, b, c, w in offsets_nb]


def halves(x):
    high = x.astype(jnp.bfloat16)
    return high, (x - high.astype(jnp.float32)).astype(jnp.bfloat16)


def split_dot(small, large, dims):
    rows = small.shape[0]
    stacked = jnp.concatenate([x.astype(jnp.float32) for x in halves(small)], axis=0).astype(jnp.bfloat16)
    total = None
    for part in halves(large):
        both = lax.dot_general(stacked, part, (dims, ((), ())), preferred_element_type=jnp.float32)
        both = both[:rows] + both[rows:]
        total = both if total is None else total + both
    return total


def lane_iota(shape):
    return lax.broadcasted_iota(jnp.int32, shape, len(shape) - 1)


def project_kernel(offsets_ref, states_ref, blocks_ref, measured_ref, weights_ref, out_ref):
    views, _, foot, pixels = blocks_ref.shape
    slices, width = states_ref.shape[1], states_ref.shape[3]
    share = measured_ref.shape[2]
    lane = lane_iota((slices, LANES))
    blocks = blocks_ref[:, 0].reshape(views * foot, pixels)
    projected = split_dot(states_ref[0, :, 0, :], blocks[:, :width], ((1,), (1,)))
    projected += split_dot(states_ref[0, :, 1, :], blocks[:, width:], ((1,), (1,)))
    step = pl.program_id(0)
    per_vreg = LANES // foot
    blank = jnp.zeros((slices, LANES - share), jnp.float32)
    for local in range(views):
        view = step * views + local
        offset = offsets_ref[0, view]
        base = offset // BLOCK
        shift = offset - base * BLOCK
        at = (local % per_vreg) * foot
        pair = projected[:, (local // per_vreg) * LANES : (local // per_vreg + 1) * LANES]
        band = jnp.where((lane >= at) & (lane < at + foot), pair, 0.0)
        band = pltpu.roll(band, (shift + LANES - at) % LANES, 1)
        first = band + jnp.concatenate([blank, measured_ref[local]], axis=1)
        second = jnp.concatenate([weights_ref[local], blank], axis=1)
        second = jnp.where(lane == share, base.astype(jnp.float32), second)
        start = view * 2 * slices
        out_ref[pl.ds(start, slices, stride=2), :] = first
        out_ref[pl.ds(start + 1, slices, stride=2), :] = second


def residual_kernel(in_ref, out_ref):
    tiles = out_ref.shape[0]
    share = BLOCK
    lane = lane_iota((tiles, LANES))
    first = in_ref[pl.ds(0, tiles, stride=2), :]
    second = in_ref[pl.ds(1, tiles, stride=2), :]
    base = second[:, share : share + 1].astype(jnp.int32)
    onehot = jnp.where(lane_iota((tiles, tiles)) == base, 1.0, 0.0)
    placed = lax.dot_general(
        onehot, first, (((0,), (0,)), ((), ())), precision=lax.Precision.HIGHEST, preferred_element_type=jnp.float32
    )
    total = placed
    for part in (1, 2):
        moved = pltpu.roll(placed, part, 0)
        total += pltpu.roll(moved, LANES - part * share, 1)
    measured = pltpu.roll(first, share, 1)
    residual = jnp.where(lane < share, second * (total - measured), 0.0)
    windows = residual
    for part in (1, 2):
        moved = pltpu.roll(residual, tiles - part, 0)
        windows += pltpu.roll(moved, part * share, 1)
    out_ref[...] = jnp.dot(onehot, windows, precision=lax.Precision.HIGHEST, preferred_element_type=jnp.float32)


def gradient_kernel(offsets_ref, windows_ref, states_ref, blocks_ref, out_ref):
    views, _, foot, pixels = blocks_ref.shape
    slices, width = states_ref.shape[1], states_ref.shape[3]
    copies = out_ref.shape[0]
    lane = lane_iota((slices, LANES))
    per_vreg = LANES // foot
    pieces = []
    for view in range(views):
        offset = offsets_ref[0, view]
        shift = offset - (offset // BLOCK) * BLOCK
        at = (view % per_vreg) * foot
        window = windows_ref[view * slices : (view + 1) * slices, :]
        window = pltpu.roll(window, (LANES + at - shift) % LANES, 1)
        if at == 0:
            pieces.append(window)
        else:
            pieces[-1] = jnp.where(lane >= at, window, pieces[-1])
    windows = jnp.concatenate(pieces, axis=1)
    blocks = blocks_ref[:, 0].reshape(views * foot, pixels)
    gradient = split_dot(windows, blocks, ((1,), (0,)))
    for row in range(2):
        at = slice(row * width, (row + 1) * width)
        reflect = states_ref[0, :, row, :] - (2.0 * STEP_SIZE) * gradient[:, at]
        for copy in range(copies):
            out_ref[copy, :, at] = reflect


def mean_kernel(in_ref, out_ref):
    count = in_ref.shape[0]
    total = in_ref[0]
    for agent in range(1, count):
        total = total + in_ref[agent]
    out_ref[...] = total * (1.0 / count)


def shifted(row, a, c):
    slices, width = row.shape
    if a:
        where = lax.broadcasted_iota(jnp.int32, row.shape, 0)
        row = pltpu.roll(row, (slices - a) % slices, 0)
        row = jnp.where(where == (slices - 1 if a > 0 else 0), 0.0, row)
    if c:
        where = lane_iota(row.shape)
        row = pltpu.roll(row, (width - c) % width, 1)
        row = jnp.where(where == (width - 1 if c > 0 else 0), 0.0, row)
    return row


def sweep_rows(rows, averages):
    table = neighbour_table()
    moved = [{(a, c): shifted(row, a, c) for a in (-1, 0, 1) for c in (-1, 0, 1)} for row in rows]
    out = []
    for index, average in enumerate(averages):
        centre = rows[index + 1]
        numerator = average
        denominator = jnp.ones_like(average)
        for a, b, c, weight_nb in table:
            neighbour = moved[index + 1 + b][(a, c)]
            differ = centre - neighbour
            powered = jnp.exp(0.4 * jnp.log(differ * differ))
            above = 1.0 + powered
            coefficient = (weight_nb + (weight_nb * QRATIO) * powered) / (above * above)
            numerator = numerator + coefficient * neighbour
            denominator = denominator + coefficient
        out.append(numerator / denominator)
    return out


def prior_kernel(mean_ref, near_ref, side_ref, states_ref, reflect_ref, new_ref, prior_ref):
    width = states_ref.shape[3]
    tile = lax.axis_index("tile")
    last = lax.axis_size("tile") - 1
    odd = tile % 2 == 1
    near = near_ref[...]
    side = side_ref[...]
    mean = mean_ref[...]
    above = jnp.where(odd, near, side)
    below = jnp.where(odd, side, near)
    above = jnp.where(tile == 0, 0.0, above)
    below = jnp.where(tile == last, 0.0, below)
    rows = [x[:, i * width : (i + 1) * width] for x in (above, mean, below) for i in range(2)]
    averages = rows
    swept = sweep_rows(rows, averages[1:5])
    swept[0] = jnp.where(tile == 0, 0.0, swept[0])
    swept[3] = jnp.where(tile == last, 0.0, swept[3])
    final = sweep_rows(swept, averages[2:4])
    for row in range(2):
        reflect = reflect_ref[0, :, row * width : (row + 1) * width]
        prior_ref[:, row, :] = final[row]
        new_ref[0, :, row, :] = (1.0 - RELAX) * states_ref[0, :, row, :] + RELAX * (2.0 * final[row] - reflect)


def halo_pairs(n_tile, n_agent, per_x):
    near, side = [], []
    for tile in range(n_tile):
        for agent in range(n_agent):
            near.append((tile * n_agent + agent, (tile ^ 1) * n_agent + agent))
    for tile in range(1, n_tile - 1, 2):
        other = tile + 1
        for agent in range(n_agent):
            crossing = tile // per_x != other // per_x
            partner = (agent + n_agent // 2) % n_agent if crossing else agent
            one, two = tile * n_agent + agent, other * n_agent + partner
            side += [(one, two), (two, one)]
    return near, side


def shards(states, footprints, offsets, measured, weights):
    n_tile = lax.axis_size("tile")
    n_agent = lax.axis_size("agent")
    _, slices, height, width = states.shape
    views, _, foot, pixels = footprints.shape
    share = measured.shape[2]
    f32 = jnp.float32

    half = views // 2
    starts = offsets.reshape(1, views)
    sent = pl.pallas_call(
        project_kernel,
        grid=(2,),
        in_specs=[
            SMEM,
            pl.BlockSpec(states.shape, lambda i: (0, 0, 0, 0)),
            pl.BlockSpec((half, 1, foot, pixels), lambda i: (i, 0, 0, 0)),
            pl.BlockSpec((half, slices, share), lambda i: (i, 0, 0)),
            pl.BlockSpec((half, slices, share), lambda i: (i, 0, 0)),
        ],
        out_specs=pl.BlockSpec((2 * n_tile, LANES), lambda i: (0, 0)),
        out_shape=near_shape(2 * n_tile, LANES),
        name="project",
    )(starts, states, footprints, measured, weights)
    bands = lax.all_to_all(sent.reshape(n_tile, 2, LANES), "tile", 0, 0, tiled=True)
    back = pl.pallas_call(
        residual_kernel,
        in_specs=[VMEM],
        out_specs=VMEM,
        out_shape=near_shape(n_tile, LANES),
        name="residual",
    )(near(bands.reshape(2 * n_tile, LANES)))
    windows = lax.all_to_all(back.reshape(n_tile, 1, LANES), "tile", 0, 0, tiled=True)
    states_near = near(states)
    copies = pl.pallas_call(
        gradient_kernel,
        in_specs=[SMEM, VMEM, VMEM, VMEM],
        out_specs=VMEM,
        out_shape=near_shape(n_agent, slices, pixels),
        name="gradient",
    )(starts, near(windows.reshape(n_tile, LANES)), states_near, near(footprints))
    reflects = lax.all_to_all(copies, "agent", 0, 0, tiled=True)
    mean = pl.pallas_call(
        mean_kernel,
        in_specs=[VMEM],
        out_specs=VMEM,
        out_shape=near_shape(slices, pixels),
        name="mean",
    )(near(reflects))
    core_pairs, side_pairs = halo_pairs(n_tile, n_agent, 16)
    side = lax.ppermute(mean, ("tile", "agent"), side_pairs)
    core = lax.ppermute(mean, ("tile", "agent"), core_pairs)
    new_states, prior = pl.pallas_call(
        prior_kernel,
        in_specs=[VMEM] * 5,
        out_specs=[VMEM, VMEM],
        out_shape=[
            jax.ShapeDtypeStruct(states.shape, f32),
            jax.ShapeDtypeStruct((slices, height, width), f32),
        ],
        name="prior",
    )(near(mean), near(core), near(side), states_near, near(copies))
    return new_states, prior


def solution(mesh):
    in_specs = (
        P("agent", None, "tile", None),
        P("agent", "tile", None, None),
        P("agent", "tile"),
        P("agent", None, "tile"),
        P("agent", None, "tile"),
    )
    out_specs = (P("agent", None, "tile", None), P(None, "tile", None))
    return jax.shard_map(shards, mesh=mesh, in_specs=in_specs, out_specs=out_specs, check_vma=False)
```

```python
import jax
import jax.numpy as jnp
from jax import lax
from jax.experimental import pallas as pl
from jax.experimental.pallas import tpu as pltpu
from jax.sharding import PartitionSpec as P

SWEEPS = 2
STEP_SIZE = 0.25
RELAX = 0.6
QRATIO = 0.6
BLOCK = 32
LANES = 128

SMEM = pl.BlockSpec(memory_space=pltpu.SMEM)
VMEM = pl.BlockSpec(memory_space=pltpu.VMEM)


def near(x):
    return pltpu.with_memory_space_constraint(x, pltpu.VMEM)


def near_shape(*shape):
    return pltpu.VMEM(shape, jnp.float32)


def neighbour_table():
    offsets_nb = []
    for a in (-1, 0, 1):
        for b in (-1, 0, 1):
            for c in (-1, 0, 1):
                if a != 0 or b != 0 or c != 0:
                    offsets_nb.append((a, b, c, 1.0 / (a * a + b * b + c * c) ** 0.5))
    total = sum((item[3] for item in offsets_nb))
    return [(a, b, c, 4.0 * w / total) for a, b, c, w in offsets_nb]


def halves(x):
    high = x.astype(jnp.bfloat16)
    return high, (x - high.astype(jnp.float32)).astype(jnp.bfloat16)


def split_dot(small, large, dims):
    rows = small.shape[0]
    stacked = jnp.concatenate([x.astype(jnp.float32) for x in halves(small)], axis=0).astype(jnp.bfloat16)
    total = None
    for part in halves(large):
        both = lax.dot_general(stacked, part, (dims, ((), ())), preferred_element_type=jnp.float32)
        both = both[:rows] + both[rows:]
        total = both if total is None else total + both
    return total


def lane_iota(shape):
    return lax.broadcasted_iota(jnp.int32, shape, len(shape) - 1)


def project_kernel(offsets_ref, states_ref, blocks_ref, measured_ref, weights_ref, out_ref):
    views, _, foot, pixels = blocks_ref.shape
    slices, width = states_ref.shape[1], states_ref.shape[3]
    share = measured_ref.shape[2]
    lane = lane_iota((slices, LANES))
    blocks = blocks_ref[:, 0].reshape(views * foot, pixels)
    projected = split_dot(states_ref[0, :, 0, :], blocks[:, :width], ((1,), (1,)))
    projected += split_dot(states_ref[0, :, 1, :], blocks[:, width:], ((1,), (1,)))
    step = pl.program_id(0)
    per_vreg = LANES // foot
    blank = jnp.zeros((slices, LANES - share), jnp.float32)
    for local in range(views):
        view = step * views + local
        offset = offsets_ref[0, view]
        base = offset // BLOCK
        shift = offset - base * BLOCK
        at = (local % per_vreg) * foot
        pair = projected[:, (local // per_vreg) * LANES : (local // per_vreg + 1) * LANES]
        band = jnp.where((lane >= at) & (lane < at + foot), pair, 0.0)
        band = pltpu.roll(band, (shift + LANES - at) % LANES, 1)
        first = band + jnp.concatenate([blank, measured_ref[local]], axis=1)
        second = jnp.concatenate([weights_ref[local], blank], axis=1)
        second = jnp.where(lane == share, base.astype(jnp.float32), second)
        start = view * 2 * slices
        out_ref[pl.ds(start, slices, stride=2), :] = first
        out_ref[pl.ds(start + 1, slices, stride=2), :] = second


def residual_kernel(in_ref, out_ref):
    tiles = out_ref.shape[0]
    share = BLOCK
    lane = lane_iota((tiles, LANES))
    first = in_ref[pl.ds(0, tiles, stride=2), :]
    second = in_ref[pl.ds(1, tiles, stride=2), :]
    base = second[:, share : share + 1].astype(jnp.int32)
    onehot = jnp.where(lane_iota((tiles, tiles)) == base, 1.0, 0.0)
    placed = lax.dot_general(
        onehot, first, (((0,), (0,)), ((), ())), precision=lax.Precision.HIGHEST, preferred_element_type=jnp.float32
    )
    total = placed
    for part in (1, 2):
        moved = pltpu.roll(placed, part, 0)
        total += pltpu.roll(moved, LANES - part * share, 1)
    measured = pltpu.roll(first, share, 1)
    residual = jnp.where(lane < share, second * (total - measured), 0.0)
    windows = residual
    for part in (1, 2):
        moved = pltpu.roll(residual, tiles - part, 0)
        windows += pltpu.roll(moved, part * share, 1)
    out_ref[...] = jnp.dot(onehot, windows, precision=lax.Precision.HIGHEST, preferred_element_type=jnp.float32)


def gradient_kernel(offsets_ref, windows_ref, states_ref, blocks_ref, out_ref):
    views, _, foot, pixels = blocks_ref.shape
    slices, width = states_ref.shape[1], states_ref.shape[3]
    lane = lane_iota((slices, LANES))
    per_vreg = LANES // foot
    pieces = []
    for view in range(views):
        offset = offsets_ref[0, view]
        shift = offset - (offset // BLOCK) * BLOCK
        at = (view % per_vreg) * foot
        window = windows_ref[view * slices : (view + 1) * slices, :]
        window = pltpu.roll(window, (LANES + at - shift) % LANES, 1)
        if at == 0:
            pieces.append(window)
        else:
            pieces[-1] = jnp.where(lane >= at, window, pieces[-1])
    windows = jnp.concatenate(pieces, axis=1)
    blocks = blocks_ref[:, 0].reshape(views * foot, pixels)
    gradient = split_dot(windows, blocks, ((1,), (0,)))
    for row in range(2):
        at = slice(row * width, (row + 1) * width)
        out_ref[:, at] = states_ref[0, :, row, :] - (2.0 * STEP_SIZE) * gradient[:, at]


def pair_kernel(in_ref, out_ref):
    total = in_ref[0] + in_ref[1]
    for copy in range(out_ref.shape[0]):
        out_ref[copy] = total


def mean_kernel(in_ref, own_ref, other_ref):
    count = in_ref.shape[0] // 2
    means = []
    for half in range(2):
        total = in_ref[half * count]
        for member in range(1, count):
            total = total + in_ref[half * count + member]
        means.append(total * (0.5 / count))
    odd = lax.axis_index("tile") % 2 == 1
    own_ref[...] = jnp.where(odd, means[1], means[0])
    other_ref[...] = jnp.where(odd, means[0], means[1])


def shifted(row, a, c):
    slices, width = row.shape
    if a:
        where = lax.broadcasted_iota(jnp.int32, row.shape, 0)
        row = pltpu.roll(row, (slices - a) % slices, 0)
        row = jnp.where(where == (slices - 1 if a > 0 else 0), 0.0, row)
    if c:
        where = lane_iota(row.shape)
        row = pltpu.roll(row, (width - c) % width, 1)
        row = jnp.where(where == (width - 1 if c > 0 else 0), 0.0, row)
    return row


def sweep_rows(rows, averages):
    table = neighbour_table()
    moved = [{(a, c): shifted(row, a, c) for a in (-1, 0, 1) for c in (-1, 0, 1)} for row in rows]
    out = []
    for index, average in enumerate(averages):
        centre = rows[index + 1]
        numerator = average
        denominator = jnp.ones_like(average)
        for a, b, c, weight_nb in table:
            neighbour = moved[index + 1 + b][(a, c)]
            differ = centre - neighbour
            powered = jnp.exp(0.4 * jnp.log(differ * differ))
            above = 1.0 + powered
            coefficient = (weight_nb + (weight_nb * QRATIO) * powered) / (above * above)
            numerator = numerator + coefficient * neighbour
            denominator = denominator + coefficient
        out.append(numerator / denominator)
    return out


def prior_kernel(mean_ref, near_ref, side_ref, states_ref, reflect_ref, new_ref, prior_ref):
    width = states_ref.shape[3]
    tile = lax.axis_index("tile")
    last = lax.axis_size("tile") - 1
    odd = tile % 2 == 1
    near = near_ref[...]
    side = side_ref[...]
    mean = mean_ref[...]
    above = jnp.where(odd, near, side)
    below = jnp.where(odd, side, near)
    above = jnp.where(tile == 0, 0.0, above)
    below = jnp.where(tile == last, 0.0, below)
    rows = [x[:, i * width : (i + 1) * width] for x in (above, mean, below) for i in range(2)]
    averages = rows
    swept = sweep_rows(rows, averages[1:5])
    swept[0] = jnp.where(tile == 0, 0.0, swept[0])
    swept[3] = jnp.where(tile == last, 0.0, swept[3])
    final = sweep_rows(swept, averages[2:4])
    for row in range(2):
        reflect = reflect_ref[:, row * width : (row + 1) * width]
        prior_ref[:, row, :] = final[row]
        new_ref[0, :, row, :] = (1.0 - RELAX) * states_ref[0, :, row, :] + RELAX * (2.0 * final[row] - reflect)


def side_pairs(n_tile, n_agent, per_x):
    pairs = []
    for tile in range(1, n_tile - 1, 2):
        other = tile + 1
        for agent in range(n_agent):
            crossing = tile // per_x != other // per_x
            partner = (agent + n_agent // 2) % n_agent if crossing else agent
            one, two = tile * n_agent + agent, other * n_agent + partner
            pairs += [(one, two), (two, one)]
    return pairs


def chip_groups(n_tile, n_agent):
    half = n_agent // 2
    return [
        [(tile + core) * n_agent + first + y for core in range(2) for y in range(half)]
        for tile in range(0, n_tile, 2)
        for first in (0, half)
    ]


def shards(states, footprints, offsets, measured, weights):
    n_tile = lax.axis_size("tile")
    n_agent = lax.axis_size("agent")
    _, slices, height, width = states.shape
    views, _, foot, pixels = footprints.shape
    share = measured.shape[2]
    f32 = jnp.float32

    half = views // 2
    starts = offsets.reshape(1, views)
    sent = pl.pallas_call(
        project_kernel,
        grid=(2,),
        in_specs=[
            SMEM,
            pl.BlockSpec(states.shape, lambda i: (0, 0, 0, 0)),
            pl.BlockSpec((half, 1, foot, pixels), lambda i: (i, 0, 0, 0)),
            pl.BlockSpec((half, slices, share), lambda i: (i, 0, 0)),
            pl.BlockSpec((half, slices, share), lambda i: (i, 0, 0)),
        ],
        out_specs=pl.BlockSpec((2 * n_tile, LANES), lambda i: (0, 0)),
        out_shape=near_shape(2 * n_tile, LANES),
        name="project",
    )(starts, states, footprints, measured, weights)
    bands = lax.all_to_all(sent.reshape(n_tile, 2, LANES), "tile", 0, 0, tiled=True)
    back = pl.pallas_call(
        residual_kernel,
        in_specs=[VMEM],
        out_specs=VMEM,
        out_shape=near_shape(n_tile, LANES),
        name="residual",
    )(near(bands.reshape(2 * n_tile, LANES)))
    windows = lax.all_to_all(back.reshape(n_tile, 1, LANES), "tile", 0, 0, tiled=True)
    states_near = near(states)
    reflect = pl.pallas_call(
        gradient_kernel,
        in_specs=[SMEM, VMEM, VMEM, VMEM],
        out_specs=VMEM,
        out_shape=near_shape(slices, pixels),
        name="gradient",
    )(starts, near(windows.reshape(n_tile, LANES)), states_near, near(footprints))
    half = n_agent // 2
    both = lax.all_gather(reflect, "agent", axis=0, axis_index_groups=[[y, half + y] for y in range(half)])
    copies = pl.pallas_call(
        pair_kernel,
        in_specs=[VMEM],
        out_specs=VMEM,
        out_shape=near_shape(n_agent, slices, pixels),
        name="pair",
    )(near(both))
    axes = ("tile", "agent")
    shares = lax.all_to_all(copies, axes, 0, 0, tiled=True, axis_index_groups=chip_groups(n_tile, n_agent))
    mean, core = pl.pallas_call(
        mean_kernel,
        in_specs=[VMEM],
        out_specs=[VMEM, VMEM],
        out_shape=[near_shape(slices, pixels), near_shape(slices, pixels)],
        name="mean",
    )(near(shares))
    side = lax.ppermute(mean, axes, side_pairs(n_tile, n_agent, 16))
    new_states, prior = pl.pallas_call(
        prior_kernel,
        in_specs=[VMEM] * 5,
        out_specs=[VMEM, VMEM],
        out_shape=[
            jax.ShapeDtypeStruct(states.shape, f32),
            jax.ShapeDtypeStruct((slices, height, width), f32),
        ],
        name="prior",
    )(near(mean), near(core), near(side), states_near, near(reflect))
    return new_states, prior


def solution(mesh):
    in_specs = (
        P("agent", None, "tile", None),
        P("agent", "tile", None, None),
        P("agent", "tile"),
        P("agent", None, "tile"),
        P("agent", None, "tile"),
    )
    out_specs = (P("agent", None, "tile", None), P(None, "tile", None))
    return jax.shard_map(shards, mesh=mesh, in_specs=in_specs, out_specs=out_specs, check_vma=False)
```

```python
import jax
import jax.numpy as jnp
from jax import lax
from jax.experimental import pallas as pl
from jax.experimental.pallas import tpu as pltpu
from jax.sharding import PartitionSpec as P

SWEEPS = 2
STEP_SIZE = 0.25
RELAX = 0.6
BLOCK = 32
LANES = 128

SMEM = pl.BlockSpec(memory_space=pltpu.SMEM)
VMEM = pl.BlockSpec(memory_space=pltpu.VMEM)
ANY = pl.BlockSpec(memory_space=pl.ANY)


def near(x):
    return pltpu.with_memory_space_constraint(x, pltpu.VMEM)


def near_shape(*shape):
    return pltpu.VMEM(shape, jnp.float32)


def neighbour_table():
    offsets_nb = []
    for a in (-1, 0, 1):
        for b in (-1, 0, 1):
            for c in (-1, 0, 1):
                if a != 0 or b != 0 or c != 0:
                    offsets_nb.append((a, b, c, 1.0 / (a * a + b * b + c * c) ** 0.5))
    total = sum((item[3] for item in offsets_nb))
    return [(a, b, c, 4.0 * w / total) for a, b, c, w in offsets_nb]


def halves(x):
    high = x.astype(jnp.bfloat16)
    return high, (x - high.astype(jnp.float32)).astype(jnp.bfloat16)


def split_dot(small, large, dims):
    rows = small.shape[0]
    stacked = jnp.concatenate([x.astype(jnp.float32) for x in halves(small)], axis=0).astype(jnp.bfloat16)
    total = None
    for part in halves(large):
        both = lax.dot_general(stacked, part, (dims, ((), ())), preferred_element_type=jnp.float32)
        both = both[:rows] + both[rows:]
        total = both if total is None else total + both
    return total


def lane_iota(shape):
    return lax.broadcasted_iota(jnp.int32, shape, len(shape) - 1)


PIECES = 4


def project_kernel(
    offsets_ref, states_hbm, blocks_hbm, measured_hbm, weights_hbm, out_ref, blocks_ref,
    states_ref, measured_ref, weights_ref, piece_sems, small_sems,
):
    views, _, foot, pixels = blocks_ref.shape
    slices, width = states_ref.shape[1], states_ref.shape[3]
    share = measured_ref.shape[2]
    per_piece = views // PIECES
    small = [
        pltpu.make_async_copy(source, target, small_sems.at[i])
        for i, (source, target) in enumerate(
            ((states_hbm, states_ref), (measured_hbm, measured_ref), (weights_hbm, weights_ref))
        )
    ]
    pieces = [
        pltpu.make_async_copy(
            blocks_hbm.at[pl.ds(i * per_piece, per_piece)], blocks_ref.at[pl.ds(i * per_piece, per_piece)], piece_sems.at[i]
        )
        for i in range(PIECES)
    ]
    small[0].start()
    pieces[0].start()
    small[1].start()
    small[2].start()
    for piece in pieces[1:]:
        piece.start()
    lane = lane_iota((slices, LANES))
    per_vreg = LANES // foot
    blank = jnp.zeros((slices, LANES - share), jnp.float32)
    for index, piece in enumerate(pieces):
        if index == 0:
            small[0].wait()
        piece.wait()
        first_view = index * per_piece
        blocks = blocks_ref[first_view : first_view + per_piece, 0].reshape(per_piece * foot, pixels)
        projected = split_dot(states_ref[0, :, 0, :], blocks[:, :width], ((1,), (1,)))
        projected += split_dot(states_ref[0, :, 1, :], blocks[:, width:], ((1,), (1,)))
        if index == 0:
            small[1].wait()
            small[2].wait()
        for local in range(per_piece):
            view = first_view + local
            offset = offsets_ref[0, view]
            base = offset // BLOCK
            shift = offset - base * BLOCK
            at = (local % per_vreg) * foot
            pair = projected[:, (local // per_vreg) * LANES : (local // per_vreg + 1) * LANES]
            band = jnp.where((lane >= at) & (lane < at + foot), pair, 0.0)
            band = pltpu.roll(band, (shift + LANES - at) % LANES, 1)
            first = band + jnp.concatenate([blank, measured_ref[view]], axis=1)
            second = jnp.concatenate([weights_ref[view], blank], axis=1)
            second = jnp.where(lane == share, base.astype(jnp.float32), second)
            start = view * 2 * slices
            out_ref[pl.ds(start, slices, stride=2), :] = first
            out_ref[pl.ds(start + 1, slices, stride=2), :] = second


def thirds(x):
    high = x.astype(jnp.bfloat16)
    rest = x - high.astype(jnp.float32)
    mid = rest.astype(jnp.bfloat16)
    low = (rest - mid.astype(jnp.float32)).astype(jnp.bfloat16)
    return jnp.concatenate([high, mid, low], axis=1)


def select_dot(onehot, x, dims):
    width = x.shape[1]
    all_three = lax.dot_general(onehot, thirds(x), (dims, ((), ())), preferred_element_type=jnp.float32)
    return all_three[:, :width] + (all_three[:, width : 2 * width] + all_three[:, 2 * width :])


def residual_kernel(in_ref, out_ref):
    tiles = out_ref.shape[0]
    share = BLOCK
    lane = lane_iota((tiles, LANES))
    first = in_ref[pl.ds(0, tiles, stride=2), :]
    second = in_ref[pl.ds(1, tiles, stride=2), :]
    base = second[:, share : share + 1].astype(jnp.int32)
    onehot = jnp.where(lane_iota((tiles, tiles)) == base, 1.0, 0.0).astype(jnp.bfloat16)
    placed = select_dot(onehot, first, ((0,), (0,)))
    total = placed
    for part in (1, 2):
        moved = pltpu.roll(placed, part, 0)
        total += pltpu.roll(moved, LANES - part * share, 1)
    measured = pltpu.roll(first, share, 1)
    residual = jnp.where(lane < share, second * (total - measured), 0.0)
    windows = residual
    for part in (1, 2):
        moved = pltpu.roll(residual, tiles - part, 0)
        windows += pltpu.roll(moved, part * share, 1)
    out_ref[...] = select_dot(onehot, windows, ((1,), (0,)))


def gradient_kernel(offsets_ref, windows_ref, states_ref, blocks_ref, out_ref):
    views, _, foot, pixels = blocks_ref.shape
    slices, width = states_ref.shape[1], states_ref.shape[3]
    lane = lane_iota((slices, LANES))
    per_vreg = LANES // foot
    pieces = []
    for view in range(views):
        offset = offsets_ref[0, view]
        shift = offset - (offset // BLOCK) * BLOCK
        at = (view % per_vreg) * foot
        window = windows_ref[view * slices : (view + 1) * slices, :]
        window = pltpu.roll(window, (LANES + at - shift) % LANES, 1)
        if at == 0:
            pieces.append(window)
        else:
            pieces[-1] = jnp.where(lane >= at, window, pieces[-1])
    windows = jnp.concatenate(pieces, axis=1)
    blocks = blocks_ref[:, 0].reshape(views * foot, pixels)
    gradient = split_dot(windows, blocks, ((1,), (0,)))
    for row in range(2):
        at = slice(row * width, (row + 1) * width)
        out_ref[:, at] = states_ref[0, :, row, :] - (2.0 * STEP_SIZE) * gradient[:, at]


def pair_kernel(in_ref, out_ref):
    total = in_ref[0] + in_ref[1]
    for copy in range(out_ref.shape[0]):
        out_ref[copy] = total


def mean_kernel(in_ref, own_ref, other_ref):
    count = in_ref.shape[0] // 2
    means = []
    for half in range(2):
        total = in_ref[half * count]
        for member in range(1, count):
            total = total + in_ref[half * count + member]
        means.append(total * (0.5 / count))
    odd = lax.axis_index("tile") % 2 == 1
    own_ref[...] = jnp.where(odd, means[1], means[0])
    other_ref[...] = jnp.where(odd, means[0], means[1])


def shifted(row, a, c):
    slices, width = row.shape
    if a:
        where = lax.broadcasted_iota(jnp.int32, row.shape, 0)
        row = pltpu.roll(row, (slices - a) % slices, 0)
        row = jnp.where(where == (slices - 1 if a > 0 else 0), 0.0, row)
    if c:
        where = lane_iota(row.shape)
        row = pltpu.roll(row, (width - c) % width, 1)
        row = jnp.where(where == (width - 1 if c > 0 else 0), 0.0, row)
    return row


def sweep_rows(rows, averages):
    table = neighbour_table()
    moved = [{(a, c): shifted(row, a, c) for a in (-1, 0, 1) for c in (-1, 0, 1)} for row in rows]
    out = []
    for index, average in enumerate(averages):
        centre = rows[index + 1]
        above, below = {}, {}
        for a, b, c, weight_nb in table:
            neighbour = moved[index + 1 + b][(a, c)]
            differ = centre - neighbour
            bend = jnp.tanh(0.2 * jnp.log(differ * differ))
            coefficient = (1.0 - bend) * (4.0 - bend)
            scaled = coefficient * neighbour
            above[weight_nb] = above[weight_nb] + scaled if weight_nb in above else scaled
            below[weight_nb] = below[weight_nb] + coefficient if weight_nb in below else coefficient
        numerator = average
        denominator = jnp.ones_like(average)
        for weight_nb in above:
            numerator = numerator + (0.1 * weight_nb) * above[weight_nb]
            denominator = denominator + (0.1 * weight_nb) * below[weight_nb]
        out.append(numerator / denominator)
    return out


def prior_kernel(mean_ref, near_ref, side_ref, states_ref, reflect_ref, new_ref, prior_ref):
    width = states_ref.shape[3]
    tile = lax.axis_index("tile")
    last = lax.axis_size("tile") - 1
    odd = tile % 2 == 1
    near = near_ref[...]
    side = side_ref[...]
    mean = mean_ref[...]
    above = jnp.where(odd, near, side)
    below = jnp.where(odd, side, near)
    above = jnp.where(tile == 0, 0.0, above)
    below = jnp.where(tile == last, 0.0, below)
    rows = [x[:, i * width : (i + 1) * width] for x in (above, mean, below) for i in range(2)]
    averages = rows
    swept = sweep_rows(rows, averages[1:5])
    swept[0] = jnp.where(tile == 0, 0.0, swept[0])
    swept[3] = jnp.where(tile == last, 0.0, swept[3])
    final = sweep_rows(swept, averages[2:4])
    for row in range(2):
        reflect = reflect_ref[:, row * width : (row + 1) * width]
        prior_ref[:, row, :] = final[row]
        new_ref[0, :, row, :] = (1.0 - RELAX) * states_ref[0, :, row, :] + RELAX * (2.0 * final[row] - reflect)


def side_pairs(n_tile, n_agent, per_x):
    pairs = []
    for tile in range(1, n_tile - 1, 2):
        other = tile + 1
        for agent in range(n_agent):
            crossing = tile // per_x != other // per_x
            partner = (agent + n_agent // 2) % n_agent if crossing else agent
            one, two = tile * n_agent + agent, other * n_agent + partner
            pairs += [(one, two), (two, one)]
    return pairs


def chip_groups(n_tile, n_agent):
    half = n_agent // 2
    return [
        [(tile + core) * n_agent + first + y for core in range(2) for y in range(half)]
        for tile in range(0, n_tile, 2)
        for first in (0, half)
    ]


def shards(states, footprints, offsets, measured, weights):
    n_tile = lax.axis_size("tile")
    n_agent = lax.axis_size("agent")
    _, slices, height, width = states.shape
    views, _, foot, pixels = footprints.shape
    share = measured.shape[2]
    f32 = jnp.float32

    starts = offsets.reshape(1, views)
    sent, blocks = pl.pallas_call(
        project_kernel,
        in_specs=[SMEM, ANY, ANY, ANY, ANY],
        out_specs=[VMEM, VMEM],
        out_shape=[near_shape(2 * n_tile, LANES), near_shape(*footprints.shape)],
        scratch_shapes=[
            pltpu.VMEM(states.shape, f32),
            pltpu.VMEM(measured.shape, f32),
            pltpu.VMEM(weights.shape, f32),
            pltpu.SemaphoreType.DMA((PIECES,)),
            pltpu.SemaphoreType.DMA((3,)),
        ],
        name="project",
    )(starts, states, footprints, measured, weights)
    bands = lax.all_to_all(sent.reshape(n_tile, 2, LANES), "tile", 0, 0, tiled=True)
    back = pl.pallas_call(
        residual_kernel,
        in_specs=[VMEM],
        out_specs=VMEM,
        out_shape=near_shape(n_tile, LANES),
        name="residual",
    )(near(bands.reshape(2 * n_tile, LANES)))
    windows = lax.all_to_all(back.reshape(n_tile, 1, LANES), "tile", 0, 0, tiled=True)
    states_near = near(states)
    reflect = pl.pallas_call(
        gradient_kernel,
        in_specs=[SMEM, VMEM, VMEM, VMEM],
        out_specs=VMEM,
        out_shape=near_shape(slices, pixels),
        name="gradient",
    )(starts, near(windows.reshape(n_tile, LANES)), states_near, near(blocks))
    half = n_agent // 2
    both = lax.all_gather(reflect, "agent", axis=0, axis_index_groups=[[y, half + y] for y in range(half)])
    copies = pl.pallas_call(
        pair_kernel,
        in_specs=[VMEM],
        out_specs=VMEM,
        out_shape=near_shape(n_agent, slices, pixels),
        name="pair",
    )(near(both))
    axes = ("tile", "agent")
    shares = lax.all_to_all(copies, axes, 0, 0, tiled=True, axis_index_groups=chip_groups(n_tile, n_agent))
    mean, core = pl.pallas_call(
        mean_kernel,
        in_specs=[VMEM],
        out_specs=[VMEM, VMEM],
        out_shape=[near_shape(slices, pixels), near_shape(slices, pixels)],
        name="mean",
    )(near(shares))
    side = lax.ppermute(mean, axes, side_pairs(n_tile, n_agent, 16))
    new_states, prior = pl.pallas_call(
        prior_kernel,
        in_specs=[VMEM] * 5,
        out_specs=[VMEM, VMEM],
        out_shape=[
            jax.ShapeDtypeStruct(states.shape, f32),
            jax.ShapeDtypeStruct((slices, height, width), f32),
        ],
        name="prior",
    )(near(mean), near(core), near(side), states_near, near(reflect))
    return new_states, prior


def solution(mesh):
    in_specs = (
        P("agent", None, "tile", None),
        P("agent", "tile", None, None),
        P("agent", "tile"),
        P("agent", None, "tile"),
        P("agent", None, "tile"),
    )
    out_specs = (P("agent", None, "tile", None), P(None, "tile", None))
    return jax.shard_map(shards, mesh=mesh, in_specs=in_specs, out_specs=out_specs, check_vma=False)
```

```python
import jax
import jax.numpy as jnp
from jax import lax
from jax.experimental import pallas as pl
from jax.experimental.pallas import tpu as pltpu
from jax.sharding import PartitionSpec as P

SWEEPS = 2
STEP_SIZE = 0.25
RELAX = 0.6
BLOCK = 32
LANES = 128

SMEM = pl.BlockSpec(memory_space=pltpu.SMEM)
VMEM = pl.BlockSpec(memory_space=pltpu.VMEM)


def near(x):
    return pltpu.with_memory_space_constraint(x, pltpu.VMEM)


def near_shape(*shape):
    return pltpu.VMEM(shape, jnp.float32)


def neighbour_table():
    offsets_nb = []
    for a in (-1, 0, 1):
        for b in (-1, 0, 1):
            for c in (-1, 0, 1):
                if a != 0 or b != 0 or c != 0:
                    offsets_nb.append((a, b, c, 1.0 / (a * a + b * b + c * c) ** 0.5))
    total = sum((item[3] for item in offsets_nb))
    return [(a, b, c, 4.0 * w / total) for a, b, c, w in offsets_nb]


def halves(x):
    high = x.astype(jnp.bfloat16)
    return high, (x - high.astype(jnp.float32)).astype(jnp.bfloat16)


def split_dot(small, large, dims):
    rows = small.shape[0]
    stacked = jnp.concatenate([x.astype(jnp.float32) for x in halves(small)], axis=0).astype(jnp.bfloat16)
    total = None
    for part in halves(large):
        both = lax.dot_general(stacked, part, (dims, ((), ())), preferred_element_type=jnp.float32)
        both = both[:rows] + both[rows:]
        total = both if total is None else total + both
    return total


def lane_iota(shape):
    return lax.broadcasted_iota(jnp.int32, shape, len(shape) - 1)


def project_kernel(offsets_ref, states_ref, blocks_ref, measured_ref, weights_ref, out_ref):
    views, _, foot, pixels = blocks_ref.shape
    slices, width = states_ref.shape[1], states_ref.shape[3]
    share = measured_ref.shape[2]
    lane = lane_iota((slices, LANES))
    blocks = blocks_ref[:, 0].reshape(views * foot, pixels)
    projected = split_dot(states_ref[0, :, 0, :], blocks[:, :width], ((1,), (1,)))
    projected += split_dot(states_ref[0, :, 1, :], blocks[:, width:], ((1,), (1,)))
    step = pl.program_id(0)
    per_vreg = LANES // foot
    blank = jnp.zeros((slices, LANES - share), jnp.float32)
    for local in range(views):
        view = step * views + local
        offset = offsets_ref[0, view]
        base = offset // BLOCK
        shift = offset - base * BLOCK
        at = (local % per_vreg) * foot
        pair = projected[:, (local // per_vreg) * LANES : (local // per_vreg + 1) * LANES]
        band = jnp.where((lane >= at) & (lane < at + foot), pair, 0.0)
        band = pltpu.roll(band, (shift + LANES - at) % LANES, 1)
        first = band + jnp.concatenate([blank, measured_ref[local]], axis=1)
        second = jnp.concatenate([weights_ref[local], blank], axis=1)
        second = jnp.where(lane == share, base.astype(jnp.float32), second)
        start = view * 2 * slices
        out_ref[pl.ds(start, slices, stride=2), :] = first
        out_ref[pl.ds(start + 1, slices, stride=2), :] = second


def thirds(x):
    high = x.astype(jnp.bfloat16)
    rest = x - high.astype(jnp.float32)
    mid = rest.astype(jnp.bfloat16)
    low = (rest - mid.astype(jnp.float32)).astype(jnp.bfloat16)
    return jnp.concatenate([high, mid, low], axis=1)


def select_dot(onehot, x, dims):
    width = x.shape[1]
    all_three = lax.dot_general(onehot, thirds(x), (dims, ((), ())), preferred_element_type=jnp.float32)
    return all_three[:, :width] + (all_three[:, width : 2 * width] + all_three[:, 2 * width :])


def residual_kernel(in_ref, out_ref):
    tiles = out_ref.shape[0]
    share = BLOCK
    lane = lane_iota((tiles, LANES))
    first = in_ref[pl.ds(0, tiles, stride=2), :]
    second = in_ref[pl.ds(1, tiles, stride=2), :]
    base = second[:, share : share + 1].astype(jnp.int32)
    onehot = jnp.where(lane_iota((tiles, tiles)) == base, 1.0, 0.0).astype(jnp.bfloat16)
    placed = select_dot(onehot, first, ((0,), (0,)))
    total = placed
    for part in (1, 2):
        moved = pltpu.roll(placed, part, 0)
        total += pltpu.roll(moved, LANES - part * share, 1)
    measured = pltpu.roll(first, share, 1)
    residual = jnp.where(lane < share, second * (total - measured), 0.0)
    windows = residual
    for part in (1, 2):
        moved = pltpu.roll(residual, tiles - part, 0)
        windows += pltpu.roll(moved, part * share, 1)
    out_ref[...] = select_dot(onehot, windows, ((1,), (0,)))


def gradient_kernel(offsets_ref, windows_ref, states_ref, blocks_ref, out_ref):
    views, _, foot, pixels = blocks_ref.shape
    slices, width = states_ref.shape[1], states_ref.shape[3]
    lane = lane_iota((slices, LANES))
    per_vreg = LANES // foot
    pieces = []
    for view in range(views):
        offset = offsets_ref[0, view]
        shift = offset - (offset // BLOCK) * BLOCK
        at = (view % per_vreg) * foot
        window = windows_ref[view * slices : (view + 1) * slices, :]
        window = pltpu.roll(window, (LANES + at - shift) % LANES, 1)
        if at == 0:
            pieces.append(window)
        else:
            pieces[-1] = jnp.where(lane >= at, window, pieces[-1])
    windows = jnp.concatenate(pieces, axis=1)
    blocks = blocks_ref[:, 0].reshape(views * foot, pixels)
    gradient = split_dot(windows, blocks, ((1,), (0,)))
    for row in range(2):
        at = slice(row * width, (row + 1) * width)
        out_ref[:, at] = states_ref[0, :, row, :] - (2.0 * STEP_SIZE) * gradient[:, at]


def pair_kernel(in_ref, out_ref):
    total = in_ref[0] + in_ref[1]
    for copy in range(out_ref.shape[0]):
        out_ref[copy] = total


def mean_kernel(in_ref, own_ref, side_ref):
    count = in_ref.shape[0] // 2
    means = []
    for half in range(2):
        total = in_ref[half * count]
        for member in range(1, count):
            total = total + in_ref[half * count + member]
        means.append(total * (0.5 / count))
    odd = lax.axis_index("tile") % 2 == 1
    own_ref[...] = jnp.where(odd, means[0], means[1])
    side_ref[...] = jnp.where(odd, means[1], means[0])


def shifted(row, a, c):
    slices, width = row.shape
    if a:
        where = lax.broadcasted_iota(jnp.int32, row.shape, 0)
        row = pltpu.roll(row, (slices - a) % slices, 0)
        row = jnp.where(where == (slices - 1 if a > 0 else 0), 0.0, row)
    if c:
        where = lane_iota(row.shape)
        row = pltpu.roll(row, (width - c) % width, 1)
        row = jnp.where(where == (width - 1 if c > 0 else 0), 0.0, row)
    return row


def sweep_rows(rows, averages):
    table = neighbour_table()
    moved = [{(a, c): shifted(row, a, c) for a in (-1, 0, 1) for c in (-1, 0, 1)} for row in rows]
    out = []
    for index, average in enumerate(averages):
        centre = rows[index + 1]
        above, below = {}, {}
        for a, b, c, weight_nb in table:
            neighbour = moved[index + 1 + b][(a, c)]
            differ = centre - neighbour
            bend = jnp.tanh(0.2 * jnp.log(differ * differ))
            coefficient = (1.0 - bend) * (4.0 - bend)
            scaled = coefficient * neighbour
            above[weight_nb] = above[weight_nb] + scaled if weight_nb in above else scaled
            below[weight_nb] = below[weight_nb] + coefficient if weight_nb in below else coefficient
        numerator = average
        denominator = jnp.ones_like(average)
        for weight_nb in above:
            numerator = numerator + (0.1 * weight_nb) * above[weight_nb]
            denominator = denominator + (0.1 * weight_nb) * below[weight_nb]
        out.append(numerator / denominator)
    return out


def prior_kernel(chip_ref, side_ref, states_ref, reflect_ref, new_ref, prior_ref):
    width = states_ref.shape[3]
    tile = lax.axis_index("tile")
    last = lax.axis_size("tile") - 1
    odd = tile % 2 == 1
    side = side_ref[...]
    even, other = chip_ref[0], chip_ref[1]
    above = jnp.where(odd, even, side)
    mean = jnp.where(odd, other, even)
    below = jnp.where(odd, side, other)
    above = jnp.where(tile == 0, 0.0, above)
    below = jnp.where(tile == last, 0.0, below)
    rows = [x[:, i * width : (i + 1) * width] for x in (above, mean, below) for i in range(2)]
    averages = rows
    swept = sweep_rows(rows, averages[1:5])
    swept[0] = jnp.where(tile == 0, 0.0, swept[0])
    swept[3] = jnp.where(tile == last, 0.0, swept[3])
    final = sweep_rows(swept, averages[2:4])
    for row in range(2):
        reflect = reflect_ref[:, row * width : (row + 1) * width]
        prior_ref[:, row, :] = final[row]
        new_ref[0, :, row, :] = (1.0 - RELAX) * states_ref[0, :, row, :] + RELAX * (2.0 * final[row] - reflect)


def facing_groups(n_tile, n_agent, per_x):
    half = n_agent // 2
    groups = []
    for odd in range(1, n_tile, 2):
        even = (odd + 1) % n_tile
        for first in (0, half):
            second = first if odd // per_x == even // per_x else half - first
            groups.append(
                [odd * n_agent + first + y for y in range(half)] + [even * n_agent + second + y for y in range(half)]
            )
    return groups


def shards(states, footprints, offsets, measured, weights):
    n_tile = lax.axis_size("tile")
    n_agent = lax.axis_size("agent")
    _, slices, height, width = states.shape
    views, _, foot, pixels = footprints.shape
    share = measured.shape[2]
    f32 = jnp.float32

    half = views // 2
    starts = offsets.reshape(1, views)
    sent = pl.pallas_call(
        project_kernel,
        grid=(2,),
        in_specs=[
            SMEM,
            pl.BlockSpec(states.shape, lambda i: (0, 0, 0, 0)),
            pl.BlockSpec((half, 1, foot, pixels), lambda i: (i, 0, 0, 0)),
            pl.BlockSpec((half, slices, share), lambda i: (i, 0, 0)),
            pl.BlockSpec((half, slices, share), lambda i: (i, 0, 0)),
        ],
        out_specs=pl.BlockSpec((2 * n_tile, LANES), lambda i: (0, 0)),
        out_shape=near_shape(2 * n_tile, LANES),
        name="project",
    )(starts, states, footprints, measured, weights)
    bands = lax.all_to_all(sent.reshape(n_tile, 2, LANES), "tile", 0, 0, tiled=True)
    back = pl.pallas_call(
        residual_kernel,
        in_specs=[VMEM],
        out_specs=VMEM,
        out_shape=near_shape(n_tile, LANES),
        name="residual",
    )(near(bands.reshape(2 * n_tile, LANES)))
    windows = lax.all_to_all(back.reshape(n_tile, 1, LANES), "tile", 0, 0, tiled=True)
    states_near = near(states)
    reflect = pl.pallas_call(
        gradient_kernel,
        in_specs=[SMEM, VMEM, VMEM, VMEM],
        out_specs=VMEM,
        out_shape=near_shape(slices, pixels),
        name="gradient",
    )(starts, near(windows.reshape(n_tile, LANES)), states_near, near(footprints))
    half = n_agent // 2
    both = lax.all_gather(reflect, "agent", axis=0, axis_index_groups=[[y, half + y] for y in range(half)])
    copies = pl.pallas_call(
        pair_kernel,
        in_specs=[VMEM],
        out_specs=VMEM,
        out_shape=near_shape(n_agent, slices, pixels),
        name="pair",
    )(near(both))
    axes = ("tile", "agent")
    shares = lax.all_to_all(copies, axes, 0, 0, tiled=True, axis_index_groups=facing_groups(n_tile, n_agent, 16))
    mean, side = pl.pallas_call(
        mean_kernel,
        in_specs=[VMEM],
        out_specs=[VMEM, VMEM],
        out_shape=[near_shape(slices, pixels), near_shape(slices, pixels)],
        name="mean",
    )(near(shares))
    chip = lax.all_gather(mean, "tile", axis=0, axis_index_groups=[[t, t + 1] for t in range(0, n_tile, 2)])
    new_states, prior = pl.pallas_call(
        prior_kernel,
        in_specs=[VMEM] * 4,
        out_specs=[VMEM, VMEM],
        out_shape=[
            jax.ShapeDtypeStruct(states.shape, f32),
            jax.ShapeDtypeStruct((slices, height, width), f32),
        ],
        name="prior",
    )(near(chip), near(side), states_near, near(reflect))
    return new_states, prior


def solution(mesh):
    in_specs = (
        P("agent", None, "tile", None),
        P("agent", "tile", None, None),
        P("agent", "tile"),
        P("agent", None, "tile"),
        P("agent", None, "tile"),
    )
    out_specs = (P("agent", None, "tile", None), P(None, "tile", None))
    return jax.shard_map(shards, mesh=mesh, in_specs=in_specs, out_specs=out_specs, check_vma=False)
```

```python
import jax
import jax.numpy as jnp
from jax import lax
from jax.experimental import pallas as pl
from jax.experimental.pallas import tpu as pltpu
from jax.sharding import PartitionSpec as P

SWEEPS = 2
STEP_SIZE = 0.25
RELAX = 0.6
BLOCK = 32
LANES = 128

SMEM = pl.BlockSpec(memory_space=pltpu.SMEM)
VMEM = pl.BlockSpec(memory_space=pltpu.VMEM)


def near(x):
    return pltpu.with_memory_space_constraint(x, pltpu.VMEM)


def near_shape(*shape):
    return pltpu.VMEM(shape, jnp.float32)


def neighbour_table():
    offsets_nb = []
    for a in (-1, 0, 1):
        for b in (-1, 0, 1):
            for c in (-1, 0, 1):
                if a != 0 or b != 0 or c != 0:
                    offsets_nb.append((a, b, c, 1.0 / (a * a + b * b + c * c) ** 0.5))
    total = sum((item[3] for item in offsets_nb))
    return [(a, b, c, 4.0 * w / total) for a, b, c, w in offsets_nb]


def halves(x):
    high = x.astype(jnp.bfloat16)
    return high, (x - high.astype(jnp.float32)).astype(jnp.bfloat16)


def split_dot(small, large, dims):
    rows = small.shape[0]
    stacked = jnp.concatenate([x.astype(jnp.float32) for x in halves(small)], axis=0).astype(jnp.bfloat16)
    total = None
    for part in halves(large):
        both = lax.dot_general(stacked, part, (dims, ((), ())), preferred_element_type=jnp.float32)
        both = both[:rows] + both[rows:]
        total = both if total is None else total + both
    return total


def lane_iota(shape):
    return lax.broadcasted_iota(jnp.int32, shape, len(shape) - 1)


def project_kernel(offsets_ref, states_ref, blocks_ref, measured_ref, weights_ref, out_ref):
    views, _, foot, pixels = blocks_ref.shape
    slices, width = states_ref.shape[1], states_ref.shape[3]
    share = measured_ref.shape[2]
    lane = lane_iota((slices, LANES))
    blocks = blocks_ref[:, 0].reshape(views * foot, pixels)
    projected = split_dot(states_ref[0, :, 0, :], blocks[:, :width], ((1,), (1,)))
    projected += split_dot(states_ref[0, :, 1, :], blocks[:, width:], ((1,), (1,)))
    step = pl.program_id(0)
    per_vreg = LANES // foot
    blank = jnp.zeros((slices, LANES - share), jnp.float32)
    for local in range(views):
        view = step * views + local
        offset = offsets_ref[0, view]
        base = offset // BLOCK
        shift = offset - base * BLOCK
        at = (local % per_vreg) * foot
        pair = projected[:, (local // per_vreg) * LANES : (local // per_vreg + 1) * LANES]
        band = jnp.where((lane >= at) & (lane < at + foot), pair, 0.0)
        band = pltpu.roll(band, (shift + LANES - at) % LANES, 1)
        first = band + jnp.concatenate([blank, measured_ref[local]], axis=1)
        second = jnp.concatenate([weights_ref[local], blank], axis=1)
        second = jnp.where(lane == share, base.astype(jnp.float32), second)
        start = view * 2 * slices
        out_ref[pl.ds(start, slices, stride=2), :] = first
        out_ref[pl.ds(start + 1, slices, stride=2), :] = second


def thirds(x):
    high = x.astype(jnp.bfloat16)
    rest = x - high.astype(jnp.float32)
    mid = rest.astype(jnp.bfloat16)
    low = (rest - mid.astype(jnp.float32)).astype(jnp.bfloat16)
    return jnp.concatenate([high, mid, low], axis=1)


def select_dot(onehot, x, dims):
    width = x.shape[1]
    all_three = lax.dot_general(onehot, thirds(x), (dims, ((), ())), preferred_element_type=jnp.float32)
    return all_three[:, :width] + (all_three[:, width : 2 * width] + all_three[:, 2 * width :])


def residual_kernel(in_ref, out_ref):
    tiles = out_ref.shape[0]
    share = BLOCK
    lane = lane_iota((tiles, LANES))
    first = in_ref[pl.ds(0, tiles, stride=2), :]
    second = in_ref[pl.ds(1, tiles, stride=2), :]
    base = second[:, share : share + 1].astype(jnp.int32)
    onehot = jnp.where(lane_iota((tiles, tiles)) == base, 1.0, 0.0).astype(jnp.bfloat16)
    placed = select_dot(onehot, first, ((0,), (0,)))
    total = placed
    for part in (1, 2):
        moved = pltpu.roll(placed, part, 0)
        total += pltpu.roll(moved, LANES - part * share, 1)
    measured = pltpu.roll(first, share, 1)
    residual = jnp.where(lane < share, second * (total - measured), 0.0)
    windows = residual
    for part in (1, 2):
        moved = pltpu.roll(residual, tiles - part, 0)
        windows += pltpu.roll(moved, part * share, 1)
    out_ref[...] = select_dot(onehot, windows, ((1,), (0,)))


def gradient_kernel(offsets_ref, windows_ref, states_ref, blocks_ref, out_ref):
    views, _, foot, pixels = blocks_ref.shape
    slices, width = states_ref.shape[1], states_ref.shape[3]
    lane = lane_iota((slices, LANES))
    per_vreg = LANES // foot
    pieces = []
    for view in range(views):
        offset = offsets_ref[0, view]
        shift = offset - (offset // BLOCK) * BLOCK
        at = (view % per_vreg) * foot
        window = windows_ref[view * slices : (view + 1) * slices, :]
        window = pltpu.roll(window, (LANES + at - shift) % LANES, 1)
        if at == 0:
            pieces.append(window)
        else:
            pieces[-1] = jnp.where(lane >= at, window, pieces[-1])
    windows = jnp.concatenate(pieces, axis=1)
    blocks = blocks_ref[:, 0].reshape(views * foot, pixels)
    gradient = split_dot(windows, blocks, ((1,), (0,)))
    for row in range(2):
        at = slice(row * width, (row + 1) * width)
        out_ref[:, at] = states_ref[0, :, row, :] - (2.0 * STEP_SIZE) * gradient[:, at]


def sum_kernel(in_ref, out_ref):
    out_ref[...] = in_ref[0] + in_ref[1]


def copy_kernel(in_ref, out_ref):
    both = in_ref[...]
    for copy in range(out_ref.shape[0]):
        out_ref[copy] = both


def shifted(row, a, c):
    slices, width = row.shape
    if a:
        where = lax.broadcasted_iota(jnp.int32, row.shape, 0)
        row = pltpu.roll(row, (slices - a) % slices, 0)
        row = jnp.where(where == (slices - 1 if a > 0 else 0), 0.0, row)
    if c:
        where = lane_iota(row.shape)
        row = pltpu.roll(row, (width - c) % width, 1)
        row = jnp.where(where == (width - 1 if c > 0 else 0), 0.0, row)
    return row


def sweep_rows(rows, averages):
    table = neighbour_table()
    moved = [{(a, c): shifted(row, a, c) for a in (-1, 0, 1) for c in (-1, 0, 1)} for row in rows]
    out = []
    for index, average in enumerate(averages):
        centre = rows[index + 1]
        above, below = {}, {}
        for a, b, c, weight_nb in table:
            neighbour = moved[index + 1 + b][(a, c)]
            differ = centre - neighbour
            bend = jnp.tanh(0.2 * jnp.log(differ * differ))
            coefficient = (1.0 - bend) * (4.0 - bend)
            scaled = coefficient * neighbour
            above[weight_nb] = above[weight_nb] + scaled if weight_nb in above else scaled
            below[weight_nb] = below[weight_nb] + coefficient if weight_nb in below else coefficient
        numerator = average
        denominator = jnp.ones_like(average)
        for weight_nb in above:
            numerator = numerator + (0.1 * weight_nb) * above[weight_nb]
            denominator = denominator + (0.1 * weight_nb) * below[weight_nb]
        out.append(numerator / denominator)
    return out


def prior_kernel(shares_ref, states_ref, reflect_ref, new_ref, prior_ref):
    width = states_ref.shape[3]
    tile = lax.axis_index("tile")
    last = lax.axis_size("tile") - 1
    odd = tile % 2 == 1
    count = shares_ref.shape[0] // 2

    def mean_of(chip, core):
        total = shares_ref[chip * count, core]
        for member in range(1, count):
            total = total + shares_ref[chip * count + member, core]
        return total * (0.5 / count)

    four = [mean_of(chip, core) for chip in range(2) for core in range(2)]
    above, mean, below = [jnp.where(odd, four[i], four[i + 1]) for i in range(3)]
    above = jnp.where(tile == 0, 0.0, above)
    below = jnp.where(tile == last, 0.0, below)
    rows = [x[:, i * width : (i + 1) * width] for x in (above, mean, below) for i in range(2)]
    averages = rows
    swept = sweep_rows(rows, averages[1:5])
    swept[0] = jnp.where(tile == 0, 0.0, swept[0])
    swept[3] = jnp.where(tile == last, 0.0, swept[3])
    final = sweep_rows(swept, averages[2:4])
    for row in range(2):
        reflect = reflect_ref[:, row * width : (row + 1) * width]
        prior_ref[:, row, :] = final[row]
        new_ref[0, :, row, :] = (1.0 - RELAX) * states_ref[0, :, row, :] + RELAX * (2.0 * final[row] - reflect)


def facing_groups(n_tile, n_agent, per_x):
    half = n_agent // 2
    groups = []
    for odd in range(1, n_tile, 2):
        even = (odd + 1) % n_tile
        for first in (0, half):
            second = first if odd // per_x == even // per_x else half - first
            groups.append(
                [odd * n_agent + first + y for y in range(half)] + [even * n_agent + second + y for y in range(half)]
            )
    return groups


def shards(states, footprints, offsets, measured, weights):
    n_tile = lax.axis_size("tile")
    n_agent = lax.axis_size("agent")
    _, slices, height, width = states.shape
    views, _, foot, pixels = footprints.shape
    share = measured.shape[2]
    f32 = jnp.float32

    half = views // 2
    starts = offsets.reshape(1, views)
    sent = pl.pallas_call(
        project_kernel,
        grid=(2,),
        in_specs=[
            SMEM,
            pl.BlockSpec(states.shape, lambda i: (0, 0, 0, 0)),
            pl.BlockSpec((half, 1, foot, pixels), lambda i: (i, 0, 0, 0)),
            pl.BlockSpec((half, slices, share), lambda i: (i, 0, 0)),
            pl.BlockSpec((half, slices, share), lambda i: (i, 0, 0)),
        ],
        out_specs=pl.BlockSpec((2 * n_tile, LANES), lambda i: (0, 0)),
        out_shape=near_shape(2 * n_tile, LANES),
        name="project",
    )(starts, states, footprints, measured, weights)
    bands = lax.all_to_all(sent.reshape(n_tile, 2, LANES), "tile", 0, 0, tiled=True)
    back = pl.pallas_call(
        residual_kernel,
        in_specs=[VMEM],
        out_specs=VMEM,
        out_shape=near_shape(n_tile, LANES),
        name="residual",
    )(near(bands.reshape(2 * n_tile, LANES)))
    windows = lax.all_to_all(back.reshape(n_tile, 1, LANES), "tile", 0, 0, tiled=True)
    states_near = near(states)
    reflect = pl.pallas_call(
        gradient_kernel,
        in_specs=[SMEM, VMEM, VMEM, VMEM],
        out_specs=VMEM,
        out_shape=near_shape(slices, pixels),
        name="gradient",
    )(starts, near(windows.reshape(n_tile, LANES)), states_near, near(footprints))
    half = n_agent // 2
    both = lax.all_gather(reflect, "agent", axis=0, axis_index_groups=[[y, half + y] for y in range(half)])
    summed = pl.pallas_call(
        sum_kernel,
        in_specs=[VMEM],
        out_specs=VMEM,
        out_shape=near_shape(slices, pixels),
        name="sum",
    )(near(both))
    chip = lax.all_gather(summed, "tile", axis=0, axis_index_groups=[[t, t + 1] for t in range(0, n_tile, 2)])
    copies = pl.pallas_call(
        copy_kernel,
        in_specs=[VMEM],
        out_specs=VMEM,
        out_shape=near_shape(n_agent, 2, slices, pixels),
        name="copies",
    )(near(chip))
    axes = ("tile", "agent")
    shares = lax.all_to_all(copies, axes, 0, 0, tiled=True, axis_index_groups=facing_groups(n_tile, n_agent, 16))
    new_states, prior = pl.pallas_call(
        prior_kernel,
        in_specs=[VMEM] * 3,
        out_specs=[VMEM, VMEM],
        out_shape=[
            jax.ShapeDtypeStruct(states.shape, f32),
            jax.ShapeDtypeStruct((slices, height, width), f32),
        ],
        name="prior",
    )(near(shares), states_near, near(reflect))
    return new_states, prior


def solution(mesh):
    in_specs = (
        P("agent", None, "tile", None),
        P("agent", "tile", None, None),
        P("agent", "tile"),
        P("agent", None, "tile"),
        P("agent", None, "tile"),
    )
    out_specs = (P("agent", None, "tile", None), P(None, "tile", None))
    return jax.shard_map(shards, mesh=mesh, in_specs=in_specs, out_specs=out_specs, check_vma=False)
```

```python
import jax
import jax.numpy as jnp
from jax import lax
from jax.experimental import pallas as pl
from jax.experimental.pallas import tpu as pltpu
from jax.sharding import PartitionSpec as P

SWEEPS = 2
STEP_SIZE = 0.25
RELAX = 0.6
BLOCK = 32
LANES = 128
MIDDLE = 40
MIDDLE_FIRST = (2, 1, 3, 0)

SMEM = pl.BlockSpec(memory_space=pltpu.SMEM)
VMEM = pl.BlockSpec(memory_space=pltpu.VMEM)


def near(x):
    return pltpu.with_memory_space_constraint(x, pltpu.VMEM)


def near_shape(*shape):
    return pltpu.VMEM(shape, jnp.float32)


def neighbour_table():
    offsets_nb = []
    for a in (-1, 0, 1):
        for b in (-1, 0, 1):
            for c in (-1, 0, 1):
                if a != 0 or b != 0 or c != 0:
                    offsets_nb.append((a, b, c, 1.0 / (a * a + b * b + c * c) ** 0.5))
    total = sum((item[3] for item in offsets_nb))
    return [(a, b, c, 4.0 * w / total) for a, b, c, w in offsets_nb]


def halves(x):
    high = x.astype(jnp.bfloat16)
    return high, (x - high.astype(jnp.float32)).astype(jnp.bfloat16)


def split_dot(small, large, dims):
    rows = small.shape[0]
    stacked = jnp.concatenate([x.astype(jnp.float32) for x in halves(small)], axis=0).astype(jnp.bfloat16)
    total = None
    for part in halves(large):
        both = lax.dot_general(stacked, part, (dims, ((), ())), preferred_element_type=jnp.float32)
        both = both[:rows] + both[rows:]
        total = both if total is None else total + both
    return total


def lane_iota(shape):
    return lax.broadcasted_iota(jnp.int32, shape, len(shape) - 1)


def project_kernel(offsets_ref, states_ref, blocks_ref, measured_ref, weights_ref, out_ref):
    views, _, foot, pixels = blocks_ref.shape
    slices, width = states_ref.shape[1], states_ref.shape[3]
    share = measured_ref.shape[2]
    lane = lane_iota((slices, LANES))
    blocks = blocks_ref[:, 0].reshape(views * foot, pixels)
    projected = split_dot(states_ref[0, :, 0, :], blocks[:, :width], ((1,), (1,)))
    projected += split_dot(states_ref[0, :, 1, :], blocks[:, width:], ((1,), (1,)))
    step = pl.program_id(0)
    per_vreg = LANES // foot
    blank = jnp.zeros((slices, LANES - share), jnp.float32)
    for local in range(views):
        view = step * views + local
        offset = offsets_ref[0, view]
        base = offset // BLOCK
        shift = offset - base * BLOCK
        at = (local % per_vreg) * foot
        pair = projected[:, (local // per_vreg) * LANES : (local // per_vreg + 1) * LANES]
        band = jnp.where((lane >= at) & (lane < at + foot), pair, 0.0)
        band = pltpu.roll(band, (shift + LANES - at) % LANES, 1)
        first = band + jnp.concatenate([blank, measured_ref[local]], axis=1)
        second = jnp.concatenate([weights_ref[local], blank], axis=1)
        second = jnp.where(lane == share, base.astype(jnp.float32), second)
        start = view * 2 * slices
        out_ref[pl.ds(start, slices, stride=2), :] = first
        out_ref[pl.ds(start + 1, slices, stride=2), :] = second


def thirds(x):
    high = x.astype(jnp.bfloat16)
    rest = x - high.astype(jnp.float32)
    mid = rest.astype(jnp.bfloat16)
    low = (rest - mid.astype(jnp.float32)).astype(jnp.bfloat16)
    return jnp.concatenate([high, mid, low], axis=1)


def select_dot(onehot, x, dims):
    width = x.shape[1]
    all_three = lax.dot_general(onehot, thirds(x), (dims, ((), ())), preferred_element_type=jnp.float32)
    return all_three[:, :width] + (all_three[:, width : 2 * width] + all_three[:, 2 * width :])


def tile_order(x):
    row = lax.broadcasted_iota(jnp.int32, x.shape, 0)
    return jnp.where(row == 0, x[MIDDLE : MIDDLE + 1], jnp.where(row == MIDDLE, x[0:1], x))


def group_order(n_tile):
    order = list(range(n_tile))
    order[0], order[MIDDLE] = MIDDLE, 0
    return order


def residual_kernel(in_ref, out_ref):
    tiles = out_ref.shape[0]
    share = BLOCK
    lane = lane_iota((tiles, LANES))
    first = in_ref[pl.ds(0, tiles, stride=2), :]
    second = in_ref[pl.ds(1, tiles, stride=2), :]
    base = second[:, share : share + 1].astype(jnp.int32)
    onehot = jnp.where(lane_iota((tiles, tiles)) == base, 1.0, 0.0).astype(jnp.bfloat16)
    placed = select_dot(onehot, first, ((0,), (0,)))
    total = placed
    for part in (1, 2):
        moved = pltpu.roll(placed, part, 0)
        total += pltpu.roll(moved, LANES - part * share, 1)
    measured = pltpu.roll(tile_order(first), share, 1)
    residual = jnp.where(lane < share, tile_order(second) * (total - measured), 0.0)
    windows = residual
    for part in (1, 2):
        moved = pltpu.roll(residual, tiles - part, 0)
        windows += pltpu.roll(moved, part * share, 1)
    out_ref[...] = select_dot(onehot, windows, ((1,), (0,)))


def gradient_kernel(offsets_ref, windows_ref, states_ref, blocks_ref, out_ref):
    views, _, foot, pixels = blocks_ref.shape
    slices, width = states_ref.shape[1], states_ref.shape[3]
    lane = lane_iota((slices, LANES))
    per_vreg = LANES // foot
    pieces = []
    for view in range(views):
        offset = offsets_ref[0, view]
        shift = offset - (offset // BLOCK) * BLOCK
        at = (view % per_vreg) * foot
        window = windows_ref[view * slices : (view + 1) * slices, :]
        window = pltpu.roll(window, (LANES + at - shift) % LANES, 1)
        if at == 0:
            pieces.append(window)
        else:
            pieces[-1] = jnp.where(lane >= at, window, pieces[-1])
    windows = jnp.concatenate(pieces, axis=1)
    blocks = blocks_ref[:, 0].reshape(views * foot, pixels)
    gradient = split_dot(windows, blocks, ((1,), (0,)))
    for row in range(2):
        at = slice(row * width, (row + 1) * width)
        out_ref[:, at] = states_ref[0, :, row, :] - (2.0 * STEP_SIZE) * gradient[:, at]


def sum_kernel(in_ref, out_ref):
    out_ref[...] = in_ref[0] + in_ref[1]


def copy_kernel(in_ref, out_ref):
    both = in_ref[...]
    for copy in range(out_ref.shape[0]):
        out_ref[copy] = both


def shifted(row, a, c):
    slices, width = row.shape
    if a:
        where = lax.broadcasted_iota(jnp.int32, row.shape, 0)
        row = pltpu.roll(row, (slices - a) % slices, 0)
        row = jnp.where(where == (slices - 1 if a > 0 else 0), 0.0, row)
    if c:
        where = lane_iota(row.shape)
        row = pltpu.roll(row, (width - c) % width, 1)
        row = jnp.where(where == (width - 1 if c > 0 else 0), 0.0, row)
    return row


def sweep_rows(rows, averages):
    table = neighbour_table()
    moved = [{(a, c): shifted(row, a, c) for a in (-1, 0, 1) for c in (-1, 0, 1)} for row in rows]
    out = []
    for index, average in enumerate(averages):
        centre = rows[index + 1]
        above, below = {}, {}
        for a, b, c, weight_nb in table:
            neighbour = moved[index + 1 + b][(a, c)]
            differ = centre - neighbour
            bend = jnp.tanh(0.2 * jnp.log(differ * differ))
            coefficient = (1.0 - bend) * (4.0 - bend)
            scaled = coefficient * neighbour
            above[weight_nb] = above[weight_nb] + scaled if weight_nb in above else scaled
            below[weight_nb] = below[weight_nb] + coefficient if weight_nb in below else coefficient
        numerator = average
        denominator = jnp.ones_like(average)
        for weight_nb in above:
            numerator = numerator + (0.1 * weight_nb) * above[weight_nb]
            denominator = denominator + (0.1 * weight_nb) * below[weight_nb]
        out.append(numerator / denominator)
    return out


def prior_kernel(shares_ref, states_ref, reflect_ref, new_ref, prior_ref):
    width = states_ref.shape[3]
    tile = lax.axis_index("tile")
    last = lax.axis_size("tile") - 1
    odd = tile % 2 == 1
    count = shares_ref.shape[0] // 2

    def mean_of(chip, core):
        total = shares_ref[chip * count, core]
        for member in range(1, count):
            total = total + shares_ref[chip * count + member, core]
        return total * (0.5 / count)

    four = [mean_of(chip, core) for chip in range(2) for core in range(2)]
    above, mean, below = [jnp.where(odd, four[i], four[i + 1]) for i in range(3)]
    above = jnp.where(tile == 0, 0.0, above)
    below = jnp.where(tile == last, 0.0, below)
    rows = [x[:, i * width : (i + 1) * width] for x in (above, mean, below) for i in range(2)]
    averages = rows
    swept = sweep_rows(rows, averages[1:5])
    swept[0] = jnp.where(tile == 0, 0.0, swept[0])
    swept[3] = jnp.where(tile == last, 0.0, swept[3])
    final = sweep_rows(swept, averages[2:4])
    for row in range(2):
        reflect = reflect_ref[:, row * width : (row + 1) * width]
        prior_ref[:, row, :] = final[row]
        new_ref[0, :, row, :] = (1.0 - RELAX) * states_ref[0, :, row, :] + RELAX * (2.0 * final[row] - reflect)


def facing_groups(n_tile, n_agent, per_x):
    half = n_agent // 2
    groups = []
    for odd in range(1, n_tile, 2):
        even = (odd + 1) % n_tile
        for first in (0, half):
            second = first if odd // per_x == even // per_x else half - first
            groups.append(
                [odd * n_agent + first + y for y in MIDDLE_FIRST] + [even * n_agent + second + y for y in MIDDLE_FIRST]
            )
    return groups


def shards(states, footprints, offsets, measured, weights):
    n_tile = lax.axis_size("tile")
    n_agent = lax.axis_size("agent")
    _, slices, height, width = states.shape
    views, _, foot, pixels = footprints.shape
    share = measured.shape[2]
    f32 = jnp.float32

    half = views // 2
    starts = offsets.reshape(1, views)
    sent = pl.pallas_call(
        project_kernel,
        grid=(2,),
        in_specs=[
            SMEM,
            pl.BlockSpec(states.shape, lambda i: (0, 0, 0, 0)),
            pl.BlockSpec((half, 1, foot, pixels), lambda i: (i, 0, 0, 0)),
            pl.BlockSpec((half, slices, share), lambda i: (i, 0, 0)),
            pl.BlockSpec((half, slices, share), lambda i: (i, 0, 0)),
        ],
        out_specs=pl.BlockSpec((2 * n_tile, LANES), lambda i: (0, 0)),
        out_shape=near_shape(2 * n_tile, LANES),
        name="project",
    )(starts, states, footprints, measured, weights)
    order = [group_order(n_tile)]
    bands = lax.all_to_all(sent.reshape(n_tile, 2, LANES), "tile", 0, 0, tiled=True, axis_index_groups=order)
    back = pl.pallas_call(
        residual_kernel,
        in_specs=[VMEM],
        out_specs=VMEM,
        out_shape=near_shape(n_tile, LANES),
        name="residual",
    )(near(bands.reshape(2 * n_tile, LANES)))
    windows = lax.all_to_all(back.reshape(n_tile, 1, LANES), "tile", 0, 0, tiled=True, axis_index_groups=order)
    states_near = near(states)
    reflect = pl.pallas_call(
        gradient_kernel,
        in_specs=[SMEM, VMEM, VMEM, VMEM],
        out_specs=VMEM,
        out_shape=near_shape(slices, pixels),
        name="gradient",
    )(starts, near(windows.reshape(n_tile, LANES)), states_near, near(footprints))
    half = n_agent // 2
    both = lax.all_gather(reflect, "agent", axis=0, axis_index_groups=[[y, half + y] for y in range(half)])
    summed = pl.pallas_call(
        sum_kernel,
        in_specs=[VMEM],
        out_specs=VMEM,
        out_shape=near_shape(slices, pixels),
        name="sum",
    )(near(both))
    chip = lax.all_gather(summed, "tile", axis=0, axis_index_groups=[[t, t + 1] for t in range(0, n_tile, 2)])
    copies = pl.pallas_call(
        copy_kernel,
        in_specs=[VMEM],
        out_specs=VMEM,
        out_shape=near_shape(n_agent, 2, slices, pixels),
        name="copies",
    )(near(chip))
    axes = ("tile", "agent")
    shares = lax.all_to_all(copies, axes, 0, 0, tiled=True, axis_index_groups=facing_groups(n_tile, n_agent, 16))
    new_states, prior = pl.pallas_call(
        prior_kernel,
        in_specs=[VMEM] * 3,
        out_specs=[VMEM, VMEM],
        out_shape=[
            jax.ShapeDtypeStruct(states.shape, f32),
            jax.ShapeDtypeStruct((slices, height, width), f32),
        ],
        name="prior",
    )(near(shares), states_near, near(reflect))
    return new_states, prior


def solution(mesh):
    in_specs = (
        P("agent", None, "tile", None),
        P("agent", "tile", None, None),
        P("agent", "tile"),
        P("agent", None, "tile"),
        P("agent", None, "tile"),
    )
    out_specs = (P("agent", None, "tile", None), P(None, "tile", None))
    return jax.shard_map(shards, mesh=mesh, in_specs=in_specs, out_specs=out_specs, check_vma=False)
```

```python
import jax
import jax.numpy as jnp
from jax import lax
from jax.experimental import pallas as pl
from jax.experimental.pallas import tpu as pltpu
from jax.sharding import PartitionSpec as P

SWEEPS = 2
STEP_SIZE = 0.25
RELAX = 0.6
BLOCK = 32
LANES = 128
FIRST_OF_HALF = (42, 22)
MIDDLE_FIRST = (2, 1, 3, 0)

SMEM = pl.BlockSpec(memory_space=pltpu.SMEM)
VMEM = pl.BlockSpec(memory_space=pltpu.VMEM)


def near(x):
    return pltpu.with_memory_space_constraint(x, pltpu.VMEM)


def near_shape(*shape):
    return pltpu.VMEM(shape, jnp.float32)


def neighbour_table():
    offsets_nb = []
    for a in (-1, 0, 1):
        for b in (-1, 0, 1):
            for c in (-1, 0, 1):
                if a != 0 or b != 0 or c != 0:
                    offsets_nb.append((a, b, c, 1.0 / (a * a + b * b + c * c) ** 0.5))
    total = sum((item[3] for item in offsets_nb))
    return [(a, b, c, 4.0 * w / total) for a, b, c, w in offsets_nb]


def halves(x):
    high = x.astype(jnp.bfloat16)
    return high, (x - high.astype(jnp.float32)).astype(jnp.bfloat16)


def split_dot(small, large, dims):
    rows = small.shape[0]
    stacked = jnp.concatenate([x.astype(jnp.float32) for x in halves(small)], axis=0).astype(jnp.bfloat16)
    total = None
    for part in halves(large):
        both = lax.dot_general(stacked, part, (dims, ((), ())), preferred_element_type=jnp.float32)
        both = both[:rows] + both[rows:]
        total = both if total is None else total + both
    return total


def lane_iota(shape):
    return lax.broadcasted_iota(jnp.int32, shape, len(shape) - 1)


def project_kernel(offsets_ref, states_ref, blocks_ref, measured_ref, weights_ref, out_ref):
    views, _, foot, pixels = blocks_ref.shape
    slices, width = states_ref.shape[1], states_ref.shape[3]
    share = measured_ref.shape[2]
    lane = lane_iota((slices, LANES))
    blocks = blocks_ref[:, 0].reshape(views * foot, pixels)
    projected = split_dot(states_ref[0, :, 0, :], blocks[:, :width], ((1,), (1,)))
    projected += split_dot(states_ref[0, :, 1, :], blocks[:, width:], ((1,), (1,)))
    step = pl.program_id(0)
    tile = lax.axis_index("tile").astype(jnp.float32)
    per_vreg = LANES // foot
    blank = jnp.zeros((slices, LANES - share), jnp.float32)
    for local in range(views):
        view = step * views + local
        offset = offsets_ref[0, view]
        base = offset // BLOCK
        shift = offset - base * BLOCK
        at = (local % per_vreg) * foot
        pair = projected[:, (local // per_vreg) * LANES : (local // per_vreg + 1) * LANES]
        band = jnp.where((lane >= at) & (lane < at + foot), pair, 0.0)
        band = pltpu.roll(band, (shift + LANES - at) % LANES, 1)
        first = band + jnp.concatenate([blank, measured_ref[local]], axis=1)
        second = jnp.concatenate([weights_ref[local], blank], axis=1)
        second = jnp.where(lane == share, base.astype(jnp.float32), second)
        second = jnp.where(lane == share + 1, tile, second)
        start = view * 2 * slices
        out_ref[pl.ds(start, slices, stride=2), :] = first
        out_ref[pl.ds(start + 1, slices, stride=2), :] = second


def thirds(x):
    high = x.astype(jnp.bfloat16)
    rest = x - high.astype(jnp.float32)
    mid = rest.astype(jnp.bfloat16)
    low = (rest - mid.astype(jnp.float32)).astype(jnp.bfloat16)
    return jnp.concatenate([high, mid, low], axis=1)


def select_dot(onehot, x, dims):
    width = x.shape[1]
    all_three = lax.dot_general(onehot, thirds(x), (dims, ((), ())), preferred_element_type=jnp.float32)
    return all_three[:, :width] + (all_three[:, width : 2 * width] + all_three[:, 2 * width :])


def group_orders(n_tile, n_agent):
    half = n_agent // 2
    groups = []
    for agent in range(n_agent):
        first = FIRST_OF_HALF[agent // half]
        rest = [tile for tile in range(n_tile) if tile != first]
        if agent >= half:
            rest = rest[::-1]
        groups.append([tile * n_agent + agent for tile in [first] + rest])
    return groups


def residual_kernel(in_ref, out_ref):
    tiles = out_ref.shape[0]
    share = BLOCK
    lane = lane_iota((tiles, LANES))
    first = in_ref[pl.ds(0, tiles, stride=2), :]
    second = in_ref[pl.ds(1, tiles, stride=2), :]
    base = second[:, share : share + 1].astype(jnp.int32)
    onehot = jnp.where(lane_iota((tiles, tiles)) == base, 1.0, 0.0).astype(jnp.bfloat16)
    placed = select_dot(onehot, first, ((0,), (0,)))
    total = placed
    for part in (1, 2):
        moved = pltpu.roll(placed, part, 0)
        total += pltpu.roll(moved, LANES - part * share, 1)
    tile = second[:, share + 1 : share + 2].astype(jnp.int32)
    place = jnp.where(lane_iota((tiles, tiles)) == tile, 1.0, 0.0).astype(jnp.bfloat16)
    ordered = select_dot(place, jnp.where(lane < share, second, first), ((0,), (0,)))
    measured = pltpu.roll(ordered, share, 1)
    residual = jnp.where(lane < share, ordered * (total - measured), 0.0)
    windows = residual
    for part in (1, 2):
        moved = pltpu.roll(residual, tiles - part, 0)
        windows += pltpu.roll(moved, part * share, 1)
    out_ref[...] = select_dot(onehot, windows, ((1,), (0,)))


def gradient_kernel(offsets_ref, windows_ref, states_ref, blocks_ref, out_ref):
    views, _, foot, pixels = blocks_ref.shape
    slices, width = states_ref.shape[1], states_ref.shape[3]
    lane = lane_iota((slices, LANES))
    per_vreg = LANES // foot
    pieces = []
    for view in range(views):
        offset = offsets_ref[0, view]
        shift = offset - (offset // BLOCK) * BLOCK
        at = (view % per_vreg) * foot
        window = windows_ref[view * slices : (view + 1) * slices, :]
        window = pltpu.roll(window, (LANES + at - shift) % LANES, 1)
        if at == 0:
            pieces.append(window)
        else:
            pieces[-1] = jnp.where(lane >= at, window, pieces[-1])
    windows = jnp.concatenate(pieces, axis=1)
    blocks = blocks_ref[:, 0].reshape(views * foot, pixels)
    gradient = split_dot(windows, blocks, ((1,), (0,)))
    for row in range(2):
        at = slice(row * width, (row + 1) * width)
        out_ref[:, at] = states_ref[0, :, row, :] - (2.0 * STEP_SIZE) * gradient[:, at]


def sum_kernel(in_ref, out_ref):
    out_ref[...] = in_ref[0] + in_ref[1]


def copy_kernel(in_ref, out_ref):
    both = in_ref[...]
    for copy in range(out_ref.shape[0]):
        out_ref[copy] = both


def shifted(row, a, c):
    slices, width = row.shape
    if a:
        where = lax.broadcasted_iota(jnp.int32, row.shape, 0)
        row = pltpu.roll(row, (slices - a) % slices, 0)
        row = jnp.where(where == (slices - 1 if a > 0 else 0), 0.0, row)
    if c:
        where = lane_iota(row.shape)
        row = pltpu.roll(row, (width - c) % width, 1)
        row = jnp.where(where == (width - 1 if c > 0 else 0), 0.0, row)
    return row


def sweep_rows(rows, averages):
    table = neighbour_table()
    moved = [{(a, c): shifted(row, a, c) for a in (-1, 0, 1) for c in (-1, 0, 1)} for row in rows]
    out = []
    for index, average in enumerate(averages):
        centre = rows[index + 1]
        above, below = {}, {}
        for a, b, c, weight_nb in table:
            neighbour = moved[index + 1 + b][(a, c)]
            differ = centre - neighbour
            bend = jnp.tanh(0.2 * jnp.log(differ * differ))
            coefficient = (1.0 - bend) * (4.0 - bend)
            scaled = coefficient * neighbour
            above[weight_nb] = above[weight_nb] + scaled if weight_nb in above else scaled
            below[weight_nb] = below[weight_nb] + coefficient if weight_nb in below else coefficient
        numerator = average
        denominator = jnp.ones_like(average)
        for weight_nb in above:
            numerator = numerator + (0.1 * weight_nb) * above[weight_nb]
            denominator = denominator + (0.1 * weight_nb) * below[weight_nb]
        out.append(numerator / denominator)
    return out


def prior_kernel(shares_ref, states_ref, reflect_ref, new_ref, prior_ref):
    width = states_ref.shape[3]
    tile = lax.axis_index("tile")
    last = lax.axis_size("tile") - 1
    odd = tile % 2 == 1
    count = shares_ref.shape[0] // 2

    def mean_of(chip, core):
        total = shares_ref[chip * count, core]
        for member in range(1, count):
            total = total + shares_ref[chip * count + member, core]
        return total * (0.5 / count)

    four = [mean_of(chip, core) for chip in range(2) for core in range(2)]
    above, mean, below = [jnp.where(odd, four[i], four[i + 1]) for i in range(3)]
    above = jnp.where(tile == 0, 0.0, above)
    below = jnp.where(tile == last, 0.0, below)
    rows = [x[:, i * width : (i + 1) * width] for x in (above, mean, below) for i in range(2)]
    averages = rows
    swept = sweep_rows(rows, averages[1:5])
    swept[0] = jnp.where(tile == 0, 0.0, swept[0])
    swept[3] = jnp.where(tile == last, 0.0, swept[3])
    final = sweep_rows(swept, averages[2:4])
    for row in range(2):
        reflect = reflect_ref[:, row * width : (row + 1) * width]
        prior_ref[:, row, :] = final[row]
        new_ref[0, :, row, :] = (1.0 - RELAX) * states_ref[0, :, row, :] + RELAX * (2.0 * final[row] - reflect)


def facing_groups(n_tile, n_agent, per_x):
    half = n_agent // 2
    groups = []
    for odd in range(1, n_tile, 2):
        even = (odd + 1) % n_tile
        for first in (0, half):
            second = first if odd // per_x == even // per_x else half - first
            groups.append(
                [odd * n_agent + first + y for y in MIDDLE_FIRST] + [even * n_agent + second + y for y in MIDDLE_FIRST]
            )
    return groups


def shards(states, footprints, offsets, measured, weights):
    n_tile = lax.axis_size("tile")
    n_agent = lax.axis_size("agent")
    _, slices, height, width = states.shape
    views, _, foot, pixels = footprints.shape
    share = measured.shape[2]
    f32 = jnp.float32

    half = views // 2
    starts = offsets.reshape(1, views)
    sent = pl.pallas_call(
        project_kernel,
        grid=(2,),
        in_specs=[
            SMEM,
            pl.BlockSpec(states.shape, lambda i: (0, 0, 0, 0)),
            pl.BlockSpec((half, 1, foot, pixels), lambda i: (i, 0, 0, 0)),
            pl.BlockSpec((half, slices, share), lambda i: (i, 0, 0)),
            pl.BlockSpec((half, slices, share), lambda i: (i, 0, 0)),
        ],
        out_specs=pl.BlockSpec((2 * n_tile, LANES), lambda i: (0, 0)),
        out_shape=near_shape(2 * n_tile, LANES),
        name="project",
    )(starts, states, footprints, measured, weights)
    axes = ("tile", "agent")
    orders = group_orders(n_tile, n_agent)
    bands = lax.all_to_all(sent.reshape(n_tile, 2, LANES), axes, 0, 0, tiled=True, axis_index_groups=orders)
    back = pl.pallas_call(
        residual_kernel,
        in_specs=[VMEM],
        out_specs=VMEM,
        out_shape=near_shape(n_tile, LANES),
        name="residual",
    )(near(bands.reshape(2 * n_tile, LANES)))
    windows = lax.all_to_all(back.reshape(n_tile, 1, LANES), axes, 0, 0, tiled=True, axis_index_groups=orders)
    states_near = near(states)
    reflect = pl.pallas_call(
        gradient_kernel,
        in_specs=[SMEM, VMEM, VMEM, VMEM],
        out_specs=VMEM,
        out_shape=near_shape(slices, pixels),
        name="gradient",
    )(starts, near(windows.reshape(n_tile, LANES)), states_near, near(footprints))
    half = n_agent // 2
    both = lax.all_gather(reflect, "agent", axis=0, axis_index_groups=[[y, half + y] for y in range(half)])
    summed = pl.pallas_call(
        sum_kernel,
        in_specs=[VMEM],
        out_specs=VMEM,
        out_shape=near_shape(slices, pixels),
        name="sum",
    )(near(both))
    chip = lax.all_gather(summed, "tile", axis=0, axis_index_groups=[[t, t + 1] for t in range(0, n_tile, 2)])
    copies = pl.pallas_call(
        copy_kernel,
        in_specs=[VMEM],
        out_specs=VMEM,
        out_shape=near_shape(n_agent, 2, slices, pixels),
        name="copies",
    )(near(chip))
    shares = lax.all_to_all(copies, axes, 0, 0, tiled=True, axis_index_groups=facing_groups(n_tile, n_agent, 16))
    new_states, prior = pl.pallas_call(
        prior_kernel,
        in_specs=[VMEM] * 3,
        out_specs=[VMEM, VMEM],
        out_shape=[
            jax.ShapeDtypeStruct(states.shape, f32),
            jax.ShapeDtypeStruct((slices, height, width), f32),
        ],
        name="prior",
    )(near(shares), states_near, near(reflect))
    return new_states, prior


def solution(mesh):
    in_specs = (
        P("agent", None, "tile", None),
        P("agent", "tile", None, None),
        P("agent", "tile"),
        P("agent", None, "tile"),
        P("agent", None, "tile"),
    )
    out_specs = (P("agent", None, "tile", None), P(None, "tile", None))
    return jax.shard_map(shards, mesh=mesh, in_specs=in_specs, out_specs=out_specs, check_vma=False)
```

```python
import jax
import jax.numpy as jnp
from jax import lax
from jax.experimental import pallas as pl
from jax.experimental.pallas import tpu as pltpu
from jax.sharding import PartitionSpec as P

SWEEPS = 2
STEP_SIZE = 0.25
RELAX = 0.6
BLOCK = 32
LANES = 128
FIRST_OF_HALF = (43, 23)
MIDDLE_FIRST = (2, 1, 3, 0)

SMEM = pl.BlockSpec(memory_space=pltpu.SMEM)
VMEM = pl.BlockSpec(memory_space=pltpu.VMEM)


def near(x):
    return pltpu.with_memory_space_constraint(x, pltpu.VMEM)


def near_shape(*shape):
    return pltpu.VMEM(shape, jnp.float32)


def neighbour_table():
    offsets_nb = []
    for a in (-1, 0, 1):
        for b in (-1, 0, 1):
            for c in (-1, 0, 1):
                if a != 0 or b != 0 or c != 0:
                    offsets_nb.append((a, b, c, 1.0 / (a * a + b * b + c * c) ** 0.5))
    total = sum((item[3] for item in offsets_nb))
    return [(a, b, c, 4.0 * w / total) for a, b, c, w in offsets_nb]


def halves(x):
    high = x.astype(jnp.bfloat16)
    return high, (x - high.astype(jnp.float32)).astype(jnp.bfloat16)


def split_dot(small, large, dims):
    rows = small.shape[0]
    stacked = jnp.concatenate([x.astype(jnp.float32) for x in halves(small)], axis=0).astype(jnp.bfloat16)
    total = None
    for part in halves(large):
        both = lax.dot_general(stacked, part, (dims, ((), ())), preferred_element_type=jnp.float32)
        both = both[:rows] + both[rows:]
        total = both if total is None else total + both
    return total


def lane_iota(shape):
    return lax.broadcasted_iota(jnp.int32, shape, len(shape) - 1)


def project_kernel(offsets_ref, states_ref, blocks_ref, measured_ref, weights_ref, out_ref):
    views, _, foot, pixels = blocks_ref.shape
    slices, width = states_ref.shape[1], states_ref.shape[3]
    share = measured_ref.shape[2]
    lane = lane_iota((slices, LANES))
    blocks = blocks_ref[:, 0].reshape(views * foot, pixels)
    projected = split_dot(states_ref[0, :, 0, :], blocks[:, :width], ((1,), (1,)))
    projected += split_dot(states_ref[0, :, 1, :], blocks[:, width:], ((1,), (1,)))
    step = pl.program_id(0)
    tile = lax.axis_index("tile").astype(jnp.float32)
    per_vreg = LANES // foot
    blank = jnp.zeros((slices, LANES - share), jnp.float32)
    for local in range(views):
        view = step * views + local
        offset = offsets_ref[0, view]
        base = offset // BLOCK
        shift = offset - base * BLOCK
        at = (local % per_vreg) * foot
        pair = projected[:, (local // per_vreg) * LANES : (local // per_vreg + 1) * LANES]
        band = jnp.where((lane >= at) & (lane < at + foot), pair, 0.0)
        band = pltpu.roll(band, (shift + LANES - at) % LANES, 1)
        first = band + jnp.concatenate([blank, measured_ref[local]], axis=1)
        second = jnp.concatenate([weights_ref[local], blank], axis=1)
        second = jnp.where(lane == share, base.astype(jnp.float32), second)
        second = jnp.where(lane == share + 1, tile, second)
        start = view * 2 * slices
        out_ref[pl.ds(start, slices, stride=2), :] = first
        out_ref[pl.ds(start + 1, slices, stride=2), :] = second


def thirds(x):
    high = x.astype(jnp.bfloat16)
    rest = x - high.astype(jnp.float32)
    mid = rest.astype(jnp.bfloat16)
    low = (rest - mid.astype(jnp.float32)).astype(jnp.bfloat16)
    return jnp.concatenate([high, mid, low], axis=1)


def select_dot(onehot, x, dims):
    width = x.shape[1]
    all_three = lax.dot_general(onehot, thirds(x), (dims, ((), ())), preferred_element_type=jnp.float32)
    return all_three[:, :width] + (all_three[:, width : 2 * width] + all_three[:, 2 * width :])


def group_orders(n_tile, n_agent):
    half = n_agent // 2
    groups = []
    for agent in range(n_agent):
        first = FIRST_OF_HALF[agent // half]
        rest = [tile for tile in range(n_tile) if tile != first]
        if agent >= half:
            rest = rest[::-1]
        groups.append([tile * n_agent + agent for tile in [first] + rest])
    return groups


def residual_kernel(in_ref, out_ref):
    tiles = out_ref.shape[0]
    share = BLOCK
    lane = lane_iota((tiles, LANES))
    first = in_ref[pl.ds(0, tiles, stride=2), :]
    second = in_ref[pl.ds(1, tiles, stride=2), :]
    base = second[:, share : share + 1].astype(jnp.int32)
    onehot = jnp.where(lane_iota((tiles, tiles)) == base, 1.0, 0.0).astype(jnp.bfloat16)
    placed = select_dot(onehot, first, ((0,), (0,)))
    total = placed
    for part in (1, 2):
        moved = pltpu.roll(placed, part, 0)
        total += pltpu.roll(moved, LANES - part * share, 1)
    tile = second[:, share + 1 : share + 2].astype(jnp.int32)
    place = jnp.where(lane_iota((tiles, tiles)) == tile, 1.0, 0.0).astype(jnp.bfloat16)
    ordered = select_dot(place, jnp.where(lane < share, second, first), ((0,), (0,)))
    measured = pltpu.roll(ordered, share, 1)
    residual = jnp.where(lane < share, ordered * (total - measured), 0.0)
    windows = residual
    for part in (1, 2):
        moved = pltpu.roll(residual, tiles - part, 0)
        windows += pltpu.roll(moved, part * share, 1)
    out_ref[...] = select_dot(onehot, windows, ((1,), (0,)))


def gradient_kernel(offsets_ref, windows_ref, states_ref, blocks_ref, out_ref):
    views, _, foot, pixels = blocks_ref.shape
    slices, width = states_ref.shape[1], states_ref.shape[3]
    lane = lane_iota((slices, LANES))
    per_vreg = LANES // foot
    pieces = []
    for view in range(views):
        offset = offsets_ref[0, view]
        shift = offset - (offset // BLOCK) * BLOCK
        at = (view % per_vreg) * foot
        window = windows_ref[view * slices : (view + 1) * slices, :]
        window = pltpu.roll(window, (LANES + at - shift) % LANES, 1)
        if at == 0:
            pieces.append(window)
        else:
            pieces[-1] = jnp.where(lane >= at, window, pieces[-1])
    windows = jnp.concatenate(pieces, axis=1)
    blocks = blocks_ref[:, 0].reshape(views * foot, pixels)
    gradient = split_dot(windows, blocks, ((1,), (0,)))
    for row in range(2):
        at = slice(row * width, (row + 1) * width)
        out_ref[:, at] = states_ref[0, :, row, :] - (2.0 * STEP_SIZE) * gradient[:, at]


def sum_kernel(in_ref, out_ref):
    out_ref[...] = in_ref[0] + in_ref[1]


def copy_kernel(in_ref, out_ref):
    both = in_ref[...]
    for copy in range(out_ref.shape[0]):
        out_ref[copy] = both


def shifted(row, a, c):
    slices, width = row.shape
    if a:
        where = lax.broadcasted_iota(jnp.int32, row.shape, 0)
        row = pltpu.roll(row, (slices - a) % slices, 0)
        row = jnp.where(where == (slices - 1 if a > 0 else 0), 0.0, row)
    if c:
        where = lane_iota(row.shape)
        row = pltpu.roll(row, (width - c) % width, 1)
        row = jnp.where(where == (width - 1 if c > 0 else 0), 0.0, row)
    return row


def sweep_rows(rows, averages):
    table = neighbour_table()
    moved = [{(a, c): shifted(row, a, c) for a in (-1, 0, 1) for c in (-1, 0, 1)} for row in rows]
    out = []
    for index, average in enumerate(averages):
        centre = rows[index + 1]
        above, below = {}, {}
        for a, b, c, weight_nb in table:
            neighbour = moved[index + 1 + b][(a, c)]
            differ = centre - neighbour
            bend = jnp.tanh(0.2 * jnp.log(differ * differ))
            coefficient = (1.0 - bend) * (4.0 - bend)
            scaled = coefficient * neighbour
            above[weight_nb] = above[weight_nb] + scaled if weight_nb in above else scaled
            below[weight_nb] = below[weight_nb] + coefficient if weight_nb in below else coefficient
        numerator = average
        denominator = jnp.ones_like(average)
        for weight_nb in above:
            numerator = numerator + (0.1 * weight_nb) * above[weight_nb]
            denominator = denominator + (0.1 * weight_nb) * below[weight_nb]
        out.append(numerator / denominator)
    return out


def prior_kernel(shares_ref, states_ref, reflect_ref, new_ref, prior_ref):
    width = states_ref.shape[3]
    tile = lax.axis_index("tile")
    last = lax.axis_size("tile") - 1
    odd = tile % 2 == 1
    count = shares_ref.shape[0] // 2

    def mean_of(chip, core):
        total = shares_ref[chip * count, core]
        for member in range(1, count):
            total = total + shares_ref[chip * count + member, core]
        return total * (0.5 / count)

    four = [mean_of(chip, core) for chip in range(2) for core in range(2)]
    above, mean, below = [jnp.where(odd, four[i], four[i + 1]) for i in range(3)]
    above = jnp.where(tile == 0, 0.0, above)
    below = jnp.where(tile == last, 0.0, below)
    rows = [x[:, i * width : (i + 1) * width] for x in (above, mean, below) for i in range(2)]
    averages = rows
    swept = sweep_rows(rows, averages[1:5])
    swept[0] = jnp.where(tile == 0, 0.0, swept[0])
    swept[3] = jnp.where(tile == last, 0.0, swept[3])
    final = sweep_rows(swept, averages[2:4])
    for row in range(2):
        reflect = reflect_ref[:, row * width : (row + 1) * width]
        prior_ref[:, row, :] = final[row]
        new_ref[0, :, row, :] = (1.0 - RELAX) * states_ref[0, :, row, :] + RELAX * (2.0 * final[row] - reflect)


def facing_groups(n_tile, n_agent, per_x):
    half = n_agent // 2
    groups = []
    for odd in range(1, n_tile, 2):
        even = (odd + 1) % n_tile
        for first in (0, half):
            second = first if odd // per_x == even // per_x else half - first
            groups.append(
                [odd * n_agent + first + y for y in MIDDLE_FIRST] + [even * n_agent + second + y for y in MIDDLE_FIRST]
            )
    return groups


def shards(states, footprints, offsets, measured, weights):
    n_tile = lax.axis_size("tile")
    n_agent = lax.axis_size("agent")
    _, slices, height, width = states.shape
    views, _, foot, pixels = footprints.shape
    share = measured.shape[2]
    f32 = jnp.float32

    half = views // 2
    starts = offsets.reshape(1, views)
    sent = pl.pallas_call(
        project_kernel,
        grid=(2,),
        in_specs=[
            SMEM,
            pl.BlockSpec(states.shape, lambda i: (0, 0, 0, 0)),
            pl.BlockSpec((half, 1, foot, pixels), lambda i: (i, 0, 0, 0)),
            pl.BlockSpec((half, slices, share), lambda i: (i, 0, 0)),
            pl.BlockSpec((half, slices, share), lambda i: (i, 0, 0)),
        ],
        out_specs=pl.BlockSpec((2 * n_tile, LANES), lambda i: (0, 0)),
        out_shape=near_shape(2 * n_tile, LANES),
        name="project",
    )(starts, states, footprints, measured, weights)
    axes = ("tile", "agent")
    orders = group_orders(n_tile, n_agent)
    bands = lax.all_to_all(sent.reshape(n_tile, 2, LANES), axes, 0, 0, tiled=True, axis_index_groups=orders)
    back = pl.pallas_call(
        residual_kernel,
        in_specs=[VMEM],
        out_specs=VMEM,
        out_shape=near_shape(n_tile, LANES),
        name="residual",
    )(near(bands.reshape(2 * n_tile, LANES)))
    windows = lax.all_to_all(back.reshape(n_tile, 1, LANES), axes, 0, 0, tiled=True, axis_index_groups=orders)
    states_near = near(states)
    reflect = pl.pallas_call(
        gradient_kernel,
        in_specs=[SMEM, VMEM, VMEM, VMEM],
        out_specs=VMEM,
        out_shape=near_shape(slices, pixels),
        name="gradient",
    )(starts, near(windows.reshape(n_tile, LANES)), states_near, near(footprints))
    half = n_agent // 2
    both = lax.all_gather(reflect, "agent", axis=0, axis_index_groups=[[y, half + y] for y in range(half)])
    summed = pl.pallas_call(
        sum_kernel,
        in_specs=[VMEM],
        out_specs=VMEM,
        out_shape=near_shape(slices, pixels),
        name="sum",
    )(near(both))
    chip = lax.all_gather(summed, "tile", axis=0, axis_index_groups=[[t, t + 1] for t in range(0, n_tile, 2)])
    copies = pl.pallas_call(
        copy_kernel,
        in_specs=[VMEM],
        out_specs=VMEM,
        out_shape=near_shape(n_agent, 2, slices, pixels),
        name="copies",
    )(near(chip))
    shares = lax.all_to_all(copies, axes, 0, 0, tiled=True, axis_index_groups=facing_groups(n_tile, n_agent, 16))
    new_states, prior = pl.pallas_call(
        prior_kernel,
        in_specs=[VMEM] * 3,
        out_specs=[VMEM, VMEM],
        out_shape=[
            jax.ShapeDtypeStruct(states.shape, f32),
            jax.ShapeDtypeStruct((slices, height, width), f32),
        ],
        name="prior",
    )(near(shares), states_near, near(reflect))
    return new_states, prior


def solution(mesh):
    in_specs = (
        P("agent", None, "tile", None),
        P("agent", "tile", None, None),
        P("agent", "tile"),
        P("agent", None, "tile"),
        P("agent", None, "tile"),
    )
    out_specs = (P("agent", None, "tile", None), P(None, "tile", None))
    return jax.shard_map(shards, mesh=mesh, in_specs=in_specs, out_specs=out_specs, check_vma=False)
```
